256 devices in a mesh: pts: 64 (over x, z, core), rep: 4 (over y).
Axes of the slice: x: 4, y: 4, z: 8, core: 2. Of those that a mesh axis runs over, the one named last changes fastest.
Arguments:
- points: bfloat16 [4, 131072, 512], P('rep', 'pts'), may hold values from -60 to 60
- counts: int32 [4, 64], P('rep', 'pts'), may hold values from 0 to 2048, as said below
- hilbert_rank: int32 [4, 131072], P('rep', 'pts'), may hold values from 0 to 65535, as said below
- patch_shift: int32 [4], P('rep'), may hold values from 1 to 1023
- norm_gain: float32 [512], replicated, may hold values from 0.1 to 1.9
- project_in: bfloat16 [512, 1536], replicated, may hold values from -8 to 8
- project_out: bfloat16 [512, 512], replicated, may hold values from -0.25 to 0.25
- cotangent: bfloat16 [4, 65536, 512], P('rep', 'pts'), may hold values from -6 to 6
Outputs:
- block_out: bfloat16 [4, 65536, 512], P('rep', 'pts')
- grad_points: bfloat16 [4, 131072, 512], P('rep', 'pts')
- grad_project_in: float32 [512, 1536], replicated
- grad_project_out: float32 [512, 512], replicated
- grad_gain: float32 [512], replicated
The draws below stay inside these ranges and needn't reach their ends.
Inputs may be any that keep to these rules, and one draw needn't show every extreme that they name: The valid points of shard d fill its first counts[b, d] slots; the counts of a scan sum to 65536, and in every scan some shard holds exactly 2048. `hilbert_rank`: the ranks of the valid slots of a scan are a permutation of 0 to 65535. At most 32 valid slots of one shard have ranks in one block [m * 1024, (m + 1) * 1024); in every scan some shard has exactly 32 in every block. Slots beyond the count hold arbitrary ranks.
All inputs are finite; a program needn't handle non-finite values.
Results may differ from the reference program's by a relative error of at most 0.012.
The reference program's roundings to bfloat16 on the way count: a program that leaves them out, or rounds other values in their place, can miss the bound.
Values may be sent and summed in bfloat16 or wider, within the bound.
A program may use at most 128 MiB of HBM per device.

```python
import math
import jax
import jax.numpy as jnp
from jax import lax

D = 512
HEADS = 8
HEAD_DIM = 64
PATCH = 1024
SCANS = 4
SHARDS = 64
ROWS = 1024
CAP = 2048
SLOT = 32
TOTAL = 65536


def scan_layout(scan_key):
    bias_key, star_key, pair_key, order_key, slot_key, filler_key = jax.random.split(scan_key, 6)
    shard_bias = jax.random.randint(bias_key, (SHARDS,), -(SLOT // 2), SLOT // 2 + 1)
    heaviest = jax.random.randint(star_key, (), 0, SHARDS)
    shard_bias = jnp.where(jnp.arange(SHARDS) == heaviest, 2 * SLOT, shard_bias)

    def one_column(column_key):
        first_key, second_key = jax.random.split(column_key)
        pairing = jax.random.permutation(first_key, SHARDS)
        first_member = pairing[0::2]
        second_member = pairing[1::2]
        jitter = jax.random.randint(second_key, (SHARDS // 2,), -(SLOT // 4), SLOT // 4 + 1)
        amount = jnp.clip(SLOT // 2 + shard_bias[first_member] - shard_bias[second_member] + jitter, 0, SLOT)
        column = jnp.zeros((SHARDS,), jnp.int32).at[first_member].set(amount)
        return column.at[second_member].set(SLOT - amount)
    pair_counts = jax.vmap(one_column)(jax.random.split(pair_key, SHARDS))
    first_index = jnp.cumsum(pair_counts, axis=1) - pair_counts
    within = jax.vmap(lambda sub_key: jax.random.permutation(sub_key, ROWS))(jax.random.split(order_key, SHARDS))
    slot_range = jnp.arange(SLOT, dtype=jnp.int32)
    wanted = jnp.clip(first_index[:, :, None] + slot_range[None, None, :], 0, ROWS - 1)
    picked = jnp.take_along_axis(within, wanted.reshape(SHARDS, SHARDS * SLOT), axis=1).reshape(SHARDS, SHARDS, SLOT)
    rank_slots = jnp.arange(SHARDS, dtype=jnp.int32)[:, None, None] * ROWS + picked
    live_slots = slot_range[None, None, :] < pair_counts[:, :, None]
    rank_slots = jnp.transpose(rank_slots, (1, 0, 2)).reshape(SHARDS, CAP)
    live_slots = jnp.transpose(live_slots, (1, 0, 2)).reshape(SHARDS, CAP)
    shuffles = jax.vmap(lambda sub_key: jax.random.permutation(sub_key, CAP))(jax.random.split(slot_key, SHARDS))
    sort_score = jnp.where(live_slots, 0, CAP) + shuffles
    arrangement = jnp.argsort(sort_score, axis=1, stable=True)
    sorted_rank = jnp.take_along_axis(rank_slots, arrangement, axis=1)
    sorted_live = jnp.take_along_axis(live_slots, arrangement, axis=1)
    filler = jax.random.randint(filler_key, (SHARDS, CAP), 0, TOTAL)
    final_rank = jnp.where(sorted_live, sorted_rank, filler).astype(jnp.int32)
    shard_counts = jnp.sum(pair_counts, axis=0).astype(jnp.int32)
    return (shard_counts, final_rank.reshape(SHARDS * CAP))


def shard_layout(base_key):
    scan_keys = jax.random.split(jax.random.fold_in(base_key, 11), SCANS)
    return jax.vmap(scan_layout)(scan_keys)


def draw_counts(key, part):
    return shard_layout(key)[0]


def draw_hilbert_rank(key, part):
    return shard_layout(key)[1]


def draw_points(key, part):
    rank_table = shard_layout(key)[1]
    value_key, column_key, row_key = jax.random.split(jax.random.fold_in(key, 23), 3)
    column_scale = jnp.exp(jax.random.uniform(column_key, (SCANS, 1, D), minval=math.log(0.3), maxval=math.log(3.0)))
    row_scale = jnp.exp(jax.random.uniform(row_key, (SCANS, TOTAL, 1), minval=math.log(0.3), maxval=math.log(3.0)))
    base = jax.random.truncated_normal(value_key, -6.0, 6.0, (SCANS, TOTAL, D)) * column_scale * row_scale
    gathered = jax.vmap(lambda base_rows, rank_row: base_rows[rank_row])(base, rank_table)
    return gathered.astype(jnp.bfloat16)


def draw_project_in(key, part):
    query_key, key_part_key, value_key = jax.random.split(jax.random.fold_in(key, 31), 3)
    scaling = D ** (-0.5)
    queries = jax.random.truncated_normal(query_key, -4.0, 4.0, (D, D)) * scaling
    values = jax.random.truncated_normal(value_key, -4.0, 4.0, (D, D)) * scaling
    noise = jax.random.truncated_normal(key_part_key, -4.0, 4.0, (D, D)) * scaling
    key_columns = noise
    return jnp.clip(jnp.concatenate([queries, key_columns, values], axis=1), -8.0, 8.0).astype(jnp.bfloat16)


def plant(array, own_key, low, top_value):
    extent = array.shape
    index_at = [jax.random.randint(jax.random.fold_in(own_key, axis), (), 0, extent[axis]) for axis in range(len(extent))]
    array = array.at[tuple(index_at)].set(low)
    longest = extent.index(max(extent))
    index_at[longest] = (index_at[longest] + 1) % extent[longest]
    return array.at[tuple(index_at)].set(top_value)


def shard_levels(stream_key, dims, shards, low, largest):
    level = 1.0
    for dim, shards_of in shards:
        heights = jax.random.uniform(jax.random.fold_in(jax.random.fold_in(stream_key, 6), dim), (shards_of,), jnp.float32, low / len(shards), largest / len(shards))
        level = level * jnp.repeat(jnp.exp(heights), dims[dim] // shards_of).reshape((-1,) + (1,) * (len(dims) - 1 - dim))
    return level


def bell_draw(key, dims, scale, limit, shards=(), kind=jnp.bfloat16):
    gain = shard_levels(key, dims, shards, -0.22, 0.18) if shards else 1.0
    drawn = jax.random.normal(key, dims, jnp.float32) * scale * gain
    return jnp.minimum(jnp.maximum(drawn, -limit), limit).astype(kind)


def setup_inputs(seed: int = 0) -> dict:
    key_list = jax.random.split(jax.random.key(seed), 9)
    points = draw_points(jax.random.fold_in(key_list[8], 71), 0)
    counts = draw_counts(jax.random.fold_in(key_list[8], 71), 0)
    hilbert_rank = draw_hilbert_rank(jax.random.fold_in(key_list[8], 71), 0)
    patch_shift = plant(jax.random.randint(key_list[3], (SCANS,), 1, PATCH), jax.random.fold_in(key_list[3], 1), 1, PATCH - 1).astype(jnp.int32)
    norm_gain = jnp.clip(1.0 + 0.18 * jax.random.normal(key_list[4], (D,), jnp.float32), 0.1, 1.9)
    project_in = draw_project_in(jax.random.fold_in(key_list[8], 71), 0)
    project_out = bell_draw(key_list[6], (D, D), D ** -0.5, 0.25)
    cotangent = bell_draw(key_list[7], (SCANS, TOTAL, D), 1.0, 6.0, ((0, 4), (1, 64)))
    return dict(points=points, counts=counts, hilbert_rank=hilbert_rank, patch_shift=patch_shift, norm_gain=norm_gain, project_in=project_in, project_out=project_out, cotangent=cotangent)


EPSILON = 1e-05

def layer_stats(rows_in):
    values = rows_in.astype(jnp.float32)
    centre = lax.optimization_barrier(jnp.mean(values, axis=-1, keepdims=True))
    deviation = values - centre
    inverse = lax.rsqrt(lax.optimization_barrier(jnp.mean(deviation * deviation, axis=-1, keepdims=True)) + EPSILON)
    return (deviation * inverse, inverse)

def patch_parts(group):
    heads_view = group.reshape(PATCH, 3, HEADS, HEAD_DIM).astype(jnp.float32)
    return (heads_view[:, 0], heads_view[:, 1], heads_view[:, 2])

def patch_forward(group):
    queries, key_rows, value_rows = patch_parts(group)
    logits = jnp.einsum('qhd,khd->hqk', queries, key_rows) * HEAD_DIM ** (-0.5)
    attention = jax.nn.softmax(logits, axis=-1).astype(jnp.bfloat16)
    attention = lax.optimization_barrier(attention).astype(jnp.float32)
    mixed_rows = jnp.einsum('hqk,khd->qhd', attention, value_rows)
    return mixed_rows.astype(jnp.bfloat16).reshape(PATCH, D)

def patch_backward(paired):
    group, grad_group = paired
    queries, key_rows, value_rows = patch_parts(group)
    logits = jnp.einsum('qhd,khd->hqk', queries, key_rows) * HEAD_DIM ** (-0.5)
    attention_f32 = jax.nn.softmax(logits, axis=-1)
    attention = lax.optimization_barrier(attention_f32.astype(jnp.bfloat16)).astype(jnp.float32)
    grad_rows = grad_group.reshape(PATCH, HEADS, HEAD_DIM).astype(jnp.float32)
    grad_values = jnp.einsum('hqk,qhd->khd', attention, grad_rows).astype(jnp.bfloat16)
    grad_attention = jnp.einsum('qhd,khd->hqk', grad_rows, value_rows)
    row_dot = lax.optimization_barrier(jnp.sum(grad_attention * attention_f32, axis=-1, keepdims=True))
    grad_logits = (attention_f32 * (grad_attention - row_dot) * HEAD_DIM ** (-0.5)).astype(jnp.bfloat16)
    grad_logits = lax.optimization_barrier(grad_logits).astype(jnp.float32)
    grad_queries = jnp.einsum('hqk,khd->qhd', grad_logits, key_rows).astype(jnp.bfloat16)
    grad_keys = jnp.einsum('hqk,qhd->khd', grad_logits, queries).astype(jnp.bfloat16)
    return jnp.stack([grad_queries, grad_keys, grad_values], axis=1).reshape(PATCH, 3 * D)

def reference(points, counts, hilbert_rank, patch_shift, norm_gain, project_in, project_out, cotangent):

    def one_scan(arguments):
        scan_points, scan_counts, scan_rank, scan_shift, scan_cot = arguments
        slot_index = jnp.arange(SHARDS * CAP, dtype=jnp.int32)
        live_slot = slot_index % CAP < scan_counts[slot_index // CAP]
        target = jnp.where(live_slot, scan_rank, TOTAL)
        ordered = jnp.zeros((TOTAL, D), jnp.bfloat16).at[target].set(scan_points, mode='drop')
        unit_rows, inverse = layer_stats(ordered)
        normed = (unit_rows * norm_gain).astype(jnp.bfloat16)
        projected = jnp.dot(normed, project_in, preferred_element_type=jnp.float32).astype(jnp.bfloat16)
        groups = jnp.roll(projected, -scan_shift, axis=0).reshape(TOTAL // PATCH, PATCH, 3 * D)
        mixed_rows = jnp.roll(lax.map(patch_forward, groups).reshape(TOTAL, D), scan_shift, axis=0)
        block_rows = (ordered.astype(jnp.float32) + jnp.dot(mixed_rows, project_out, preferred_element_type=jnp.float32)).astype(jnp.bfloat16)
        grad_mixed = jnp.dot(scan_cot, project_out.T, preferred_element_type=jnp.float32).astype(jnp.bfloat16)
        grad_out = jnp.dot(mixed_rows.T, scan_cot, preferred_element_type=jnp.float32)
        grad_groups = jnp.roll(grad_mixed, -scan_shift, axis=0).reshape(TOTAL // PATCH, PATCH, D)
        grad_projected = lax.map(patch_backward, (groups, grad_groups)).reshape(TOTAL, 3 * D)
        grad_projected = jnp.roll(grad_projected, scan_shift, axis=0)
        grad_in = jnp.dot(normed.T, grad_projected, preferred_element_type=jnp.float32)
        grad_normed = jnp.dot(grad_projected, project_in.T, preferred_element_type=jnp.float32)
        grad_scale = lax.optimization_barrier(jnp.sum(grad_normed * unit_rows, axis=0))
        weighted = grad_normed * norm_gain
        branch = inverse * (weighted - lax.optimization_barrier(jnp.mean(weighted, axis=-1, keepdims=True)) - unit_rows * lax.optimization_barrier(jnp.mean(weighted * unit_rows, axis=-1, keepdims=True)))
        grad_ordered = (scan_cot.astype(jnp.float32) + branch).astype(jnp.bfloat16)
        fetched = grad_ordered[jnp.clip(scan_rank, 0, TOTAL - 1)]
        grad_rows = jnp.where(live_slot[:, None], fetched, jnp.zeros_like(fetched))
        return (block_rows, grad_rows, grad_in, grad_out, grad_scale)
    results = lax.map(one_scan, (points, counts, hilbert_rank, patch_shift, cotangent))
    factor = 1.0 / math.sqrt(SCANS * TOTAL)
    return (results[0], results[1], lax.optimization_barrier(jnp.sum(results[2], axis=0)) * factor, lax.optimization_barrier(jnp.sum(results[3], axis=0)) * factor, lax.optimization_barrier(jnp.sum(results[4], axis=0)) * factor)
```

```python
import functools
import math

import jax
import jax.numpy as jnp
from jax import lax
from jax.experimental import pallas as pl
from jax.experimental.pallas import tpu as pltpu
from jax.sharding import PartitionSpec as P

HEAD_DIM = 64
PATCH = 1024
EPSILON = 1e-05
MESH = pl.DeviceIdType.MESH
BF16 = jnp.bfloat16
F32 = jnp.float32
NT = (((1,), (1,)), ((), ()))
TN = (((0,), (0,)), ((), ()))


def params(**kw):
    return pltpu.CompilerParams(vmem_limit_bytes=56 << 20, **kw)


def shifted(value, axis, steps):
    count = lax.axis_size(axis)
    pairs = [(source, (source + steps) % count) for source in range(count)]
    return lax.ppermute(value, axis, pairs)


def place_kernel(dest_ref, src_ref, out_ref):
    block, depth = out_ref.shape[0], src_ref.shape[0]
    row = lax.broadcasted_iota(jnp.int32, (block, depth), 0) + pl.program_id(0) * block
    hot = jnp.where(row == dest_ref[...], 1.0, 0.0).astype(BF16)
    out_ref[...] = jnp.dot(hot, src_ref[...], preferred_element_type=F32).astype(BF16)


def place(dest, src, rows, block=256):
    depth, width = src.shape
    return pl.pallas_call(
        place_kernel,
        grid=(rows // block,),
        in_specs=[
            pl.BlockSpec((1, depth), lambda i: (0, 0)),
            pl.BlockSpec((depth, width), lambda i: (0, 0)),
        ],
        out_specs=pl.BlockSpec((block, width), lambda i: (i, 0)),
        out_shape=jax.ShapeDtypeStruct((rows, width), BF16),
        compiler_params=params(),
        name="place",
    )(dest.reshape(1, depth), src)


def fetch_kernel(index_ref, src_ref, out_ref):
    block, depth = out_ref.shape[0], src_ref.shape[0]
    column = lax.broadcasted_iota(jnp.int32, (block, depth), 1)
    hot = jnp.where(column == index_ref[...], 1.0, 0.0).astype(BF16)
    out_ref[...] = jnp.dot(hot, src_ref[...], preferred_element_type=F32).astype(BF16)


def fetch(index, src, block=256):
    depth, width = src.shape
    rows = index.shape[0]
    return pl.pallas_call(
        fetch_kernel,
        grid=(rows // block,),
        in_specs=[
            pl.BlockSpec((block, 1), lambda i: (i, 0)),
            pl.BlockSpec((depth, width), lambda i: (0, 0)),
        ],
        out_specs=pl.BlockSpec((block, width), lambda i: (i, 0)),
        out_shape=jax.ShapeDtypeStruct((rows, width), BF16),
        compiler_params=params(),
        name="fetch",
    )(index.reshape(rows, 1), src)


def unit_of(values):
    centre = jnp.mean(values, axis=-1, keepdims=True)
    deviation = values - centre
    inverse = lax.rsqrt(jnp.mean(deviation * deviation, axis=-1, keepdims=True) + EPSILON)
    return deviation * inverse, inverse


def project_kernel(limit_ref, own_ref, next_ref, gain_ref, weight_ref, win_ref, normed_ref, qkv_ref):
    block = own_ref.shape[0]
    row = lax.broadcasted_iota(jnp.int32, own_ref.shape, 0) + pl.program_id(0) * block
    values = jnp.where(
        row < limit_ref[0], own_ref[...].astype(F32), next_ref[...].astype(F32)
    )
    unit, _ = unit_of(values)
    normed = (unit * gain_ref[...]).astype(BF16)
    win_ref[...] = values.astype(BF16)
    normed_ref[...] = normed
    qkv_ref[...] = jnp.dot(normed, weight_ref[...], preferred_element_type=F32).astype(BF16)


def project(limit, own, following, gain, weight, block=256):
    rows, width = own.shape
    wide = weight.shape[1]
    tile = pl.BlockSpec((block, width), lambda i: (i, 0))
    return pl.pallas_call(
        project_kernel,
        grid=(rows // block,),
        in_specs=[
            pl.BlockSpec(memory_space=pltpu.SMEM),
            tile,
            tile,
            pl.BlockSpec((1, width), lambda i: (0, 0)),
            pl.BlockSpec((width, wide), lambda i: (0, 0)),
        ],
        out_specs=[tile, tile, pl.BlockSpec((block, wide), lambda i: (i, 0))],
        out_shape=[
            jax.ShapeDtypeStruct((rows, width), BF16),
            jax.ShapeDtypeStruct((rows, width), BF16),
            jax.ShapeDtypeStruct((rows, wide), BF16),
        ],
        compiler_params=params(),
        name="project",
    )(limit, own, following, gain.reshape(1, width), weight)


def attend_kernel(q_ref, k_ref, v_ref, g_ref, mixed_ref, d_ref, dk_ref, dv_ref, *, chunk):
    keys, values = k_ref[...], v_ref[...]
    lane = lax.broadcasted_iota(jnp.int32, (1, 128), 1)
    line = lax.broadcasted_iota(jnp.int32, (128, 1), 0)
    lanes = [jnp.where(lane < HEAD_DIM, 1.0, 0.0), jnp.where(lane < HEAD_DIM, 0.0, 1.0)]
    lines = [jnp.where(line < HEAD_DIM, 1.0, 0.0), jnp.where(line < HEAD_DIM, 0.0, 1.0)]
    keys_t = keys.astype(F32).T
    values_t = values.astype(F32).T
    keys_t = [(keys_t * m).astype(BF16) for m in lines]
    values_t = [(values_t * m).astype(BF16) for m in lines]
    dk_ref[...] = jnp.zeros_like(dk_ref)
    dv_ref[...] = jnp.zeros_like(dv_ref)

    def step(at, carry):
        window = pl.ds(pl.multiple_of(at * chunk, chunk), chunk)
        q_all = q_ref[window, :].astype(F32) * HEAD_DIM ** (-0.5)
        g_all = g_ref[window, :].astype(F32)
        mixed_t = jnp.zeros((128, chunk), F32)
        dq_t = jnp.zeros((128, chunk), F32)
        for head in range(2):
            q = (q_all * lanes[head]).astype(BF16)
            g = (g_all * lanes[head]).astype(BF16)
            logits = lax.dot_general(keys, q, NT, preferred_element_type=F32)
            power = jnp.exp(logits - jnp.max(logits, axis=0, keepdims=True))
            share = power * (1.0 / jnp.sum(power, axis=0, keepdims=True))
            share_b = share.astype(BF16)
            mixed_t += jnp.dot(values_t[head], share_b, preferred_element_type=F32)
            dv_ref[...] += jnp.dot(share_b, g, preferred_element_type=F32)
            dshare = lax.dot_general(values, g, NT, preferred_element_type=F32)
            dot = jnp.sum(dshare * share, axis=0, keepdims=True)
            dlogits = (share * (dshare - dot)).astype(BF16)
            dq_t += jnp.dot(keys_t[head], dlogits, preferred_element_type=F32)
            dk_ref[...] += jnp.dot(dlogits, q, preferred_element_type=F32)
        mixed_ref[window, :] = mixed_t.T.astype(BF16)
        d_ref[0, window, :] = (dq_t * HEAD_DIM ** (-0.5)).T.astype(BF16)
        return carry

    lax.fori_loop(0, q_ref.shape[0] // chunk, step, 0)
    d_ref[1] = dk_ref[...].astype(BF16)
    d_ref[2] = dv_ref[...].astype(BF16)


def attend(qkv, grads, chunk=256):
    rows, width = grads.shape
    pairs = width // 128
    return pl.pallas_call(
        functools.partial(attend_kernel, chunk=chunk),
        grid=(pairs,),
        in_specs=[
            pl.BlockSpec((rows, 128), lambda j: (0, j)),
            pl.BlockSpec((rows, 128), lambda j: (0, pairs + j)),
            pl.BlockSpec((rows, 128), lambda j: (0, 2 * pairs + j)),
            pl.BlockSpec((rows, 128), lambda j: (0, j)),
        ],
        out_specs=[
            pl.BlockSpec((rows, 128), lambda j: (0, j)),
            pl.BlockSpec((3, rows, 128), lambda j: (0, 0, j)),
        ],
        out_shape=[
            jax.ShapeDtypeStruct((rows, width), BF16),
            jax.ShapeDtypeStruct((3, rows, width), BF16),
        ],
        scratch_shapes=[pltpu.VMEM((rows, 128), F32), pltpu.VMEM((rows, 128), F32)],
        compiler_params=params(),
        name="attend",
    )(qkv, qkv, qkv, grads)


def input_grad_kernel(d_ref, weight_ref, win_ref, cot_ref, gain_ref, out_ref, scale_ref):
    width = win_ref.shape[1]
    grad = jnp.zeros(win_ref.shape, F32)
    for part in range(3):
        grad += lax.dot_general(
            d_ref[part],
            weight_ref[:, part * width : (part + 1) * width],
            NT,
            preferred_element_type=F32,
        )
    unit, inverse = unit_of(win_ref[...].astype(F32))
    product = grad * unit

    @pl.when(pl.program_id(0) == 0)
    def _():
        scale_ref[...] = jnp.zeros_like(scale_ref)

    scale_ref[...] += jnp.sum(product, axis=0, keepdims=True)
    weighted = grad * gain_ref[...]
    branch = inverse * (
        weighted
        - jnp.mean(weighted, axis=-1, keepdims=True)
        - unit * jnp.mean(product * gain_ref[...], axis=-1, keepdims=True)
    )
    out_ref[...] = (cot_ref[...].astype(F32) + branch).astype(BF16)


def input_grad(d, weight, win, cot, gain, block=256):
    rows, width = win.shape
    tile = pl.BlockSpec((block, width), lambda i: (i, 0))
    return pl.pallas_call(
        input_grad_kernel,
        grid=(rows // block,),
        in_specs=[
            pl.BlockSpec((3, block, width), lambda i: (0, i, 0)),
            pl.BlockSpec(weight.shape, lambda i: (0, 0)),
            tile,
            tile,
            pl.BlockSpec((1, width), lambda i: (0, 0)),
        ],
        out_specs=[tile, pl.BlockSpec((1, width), lambda i: (0, 0))],
        out_shape=[
            jax.ShapeDtypeStruct((rows, width), BF16),
            jax.ShapeDtypeStruct((1, width), F32),
        ],
        compiler_params=params(),
        name="input_grad",
    )(d, weight, win, cot, gain.reshape(1, width))


def weight_grad_kernel(normed_ref, d_ref, mixed_ref, cot_ref, out_ref):
    @pl.when(pl.program_id(0) < 3)
    def _():
        out_ref[...] = lax.dot_general(
            normed_ref[...], d_ref[0], TN, preferred_element_type=F32
        ).astype(BF16)

    @pl.when(pl.program_id(0) == 3)
    def _():
        out_ref[...] = lax.dot_general(
            mixed_ref[...], cot_ref[...], TN, preferred_element_type=F32
        ).astype(BF16)


def weight_grad(normed, d, mixed, cot):
    rows, width = normed.shape
    whole = pl.BlockSpec((rows, width), lambda j: (0, 0))
    return pl.pallas_call(
        weight_grad_kernel,
        grid=(4,),
        in_specs=[
            whole,
            pl.BlockSpec((1, rows, width), lambda j: (jnp.minimum(j, 2), 0, 0)),
            whole,
            whole,
        ],
        out_specs=pl.BlockSpec((width, width), lambda j: (0, j)),
        out_shape=jax.ShapeDtypeStruct((width, 4 * width), BF16),
        compiler_params=params(),
        name="weight_grad",
    )(normed, d, mixed, cot)


def reduce_kernel(
    sizes, g_ref, s_ref, out_ref, t_ref,
    half, in_core, quarter, in_y, band, in_z, piece, in_x,
    small, small_core, small_y, small_z, small_x, send_sem, recv_sem, small_send, small_recv,
):
    nx, ny, nz = sizes
    rows, wide = g_ref.shape
    half_w, part_w = wide // 2, wide // 2 // ny
    band_h, piece_h = rows // nz, rows // nz // nx
    me = lax.axis_index("pts")
    y = lax.axis_index("rep")
    core = lax.rem(me, 2)
    z = lax.rem(me // 2, nz)
    x = me // (2 * nz)

    def at(x_, y_, z_, core_):
        return {"pts": (x_ * nz + z_) * 2 + core_, "rep": y_}

    by_core = [(at(x, y, z, 1 - core), 1 - core)]
    by_y = [(at(x, lax.rem(y + k, ny), z, core), lax.rem(y + k, ny)) for k in range(1, ny)]
    by_z = [(at(x, y, lax.rem(z + k, nz), core), lax.rem(z + k, nz)) for k in range(1, nz)]
    by_x = [(at(lax.rem(x + k, nx), y, z, core), lax.rem(x + k, nx)) for k in range(1, nx)]
    everyone = by_core + by_y + by_z + by_x
    barrier = pltpu.get_barrier_semaphore()
    for device, _ in everyone:
        pl.semaphore_signal(barrier, inc=1, device_id=device, device_id_type=MESH)
    pl.semaphore_wait(barrier, len(everyone))

    def send(src, dst, slot, device, sems=(send_sem, recv_sem)):
        copy = pltpu.make_async_remote_copy(
            src_ref=src, dst_ref=dst, send_sem=sems[0].at[slot], recv_sem=sems[1].at[slot],
            device_id=device, device_id_type=MESH,
        )
        copy.start()
        return copy

    def columns(index, width, base=0):
        return pl.ds(pl.multiple_of(base + index * width, width), width)

    def lines(index, height):
        return pl.ds(pl.multiple_of(index * height, height), height)

    used = [0]

    def exchange(peers, pick, land, small_slots, mine):
        small_slots[mine] = small[...]
        copies = []
        for k, (device, index) in enumerate(peers):
            slot = used[0] + k
            copies.append(send(pick(index), land(k), slot, device))
            copies.append(send(small, small_slots.at[mine], slot, device, (small_send, small_recv)))
        used[0] += len(peers)
        for copy in copies:
            copy.wait()
        total = small_slots[0]
        for k in range(1, len(peers) + 1):
            total += small_slots[k]
        small[...] = total

    small[...] = s_ref[...]
    exchange(by_core, lambda i: g_ref.at[:, columns(i, half_w)], lambda k: in_core, small_core, core)
    own = g_ref[:, columns(core, half_w)]
    half[...] = (own.astype(F32) + in_core[...].astype(F32)).astype(BF16)
    exchange(by_y, lambda i: half.at[:, columns(i, part_w)], lambda k: in_y.at[k], small_y, y)
    total = half[:, columns(y, part_w)].astype(F32)
    for k in range(ny - 1):
        total += in_y[k].astype(F32)
    quarter[...] = total.astype(BF16)
    exchange(by_z, lambda i: quarter.at[lines(i, band_h), :], lambda k: in_z.at[k], small_z, z)
    total = quarter[lines(z, band_h), :].astype(F32)
    for k in range(nz - 1):
        total += in_z[k].astype(F32)
    band[...] = total.astype(BF16)
    exchange(by_x, lambda i: band.at[lines(i, piece_h), :], lambda k: in_x.at[k], small_x, x)
    total = band[lines(x, piece_h), :].astype(F32)
    for k in range(nx - 1):
        total += in_x[k].astype(F32)
    t_ref[...] = small[...]

    column = columns(core * ny + y, part_w)
    first = pl.multiple_of(z * band_h + x * piece_h, piece_h)
    out_ref[pl.ds(first, piece_h), column] = total.astype(BF16)

    def spread(peers, view):
        copies = [send(view, view, used[0] + k, device) for k, (device, _) in enumerate(peers)]
        used[0] += len(peers)
        for copy in copies:
            copy.wait()

    spread(by_x, out_ref.at[pl.ds(first, piece_h), column])
    spread(by_z, out_ref.at[lines(z, band_h), column])
    spread(by_y, out_ref.at[:, column])
    spread(by_core, out_ref.at[:, columns(core, half_w)])


def reduce_all(grads, small, sizes):
    nx, ny, nz = sizes
    rows, wide = grads.shape
    peers = 1 + (ny - 1) + (nz - 1) + (nx - 1)
    part = wide // 2 // ny
    vmem = pl.BlockSpec(memory_space=pltpu.VMEM)
    buffers = [
        (rows, wide // 2), (rows, wide // 2),
        (rows, part), (ny - 1, rows, part),
        (rows // nz, part), (nz - 1, rows // nz, part),
        (rows // nz // nx, part), (nx - 1, rows // nz // nx, part),
    ]
    return pl.pallas_call(
        functools.partial(reduce_kernel, sizes),
        in_specs=[vmem, vmem],
        out_specs=[vmem, vmem],
        out_shape=[
            jax.ShapeDtypeStruct(grads.shape, BF16),
            jax.ShapeDtypeStruct(small.shape, F32),
        ],
        scratch_shapes=[pltpu.VMEM(shape, BF16) for shape in buffers]
        + [pltpu.VMEM(small.shape, F32)]
        + [pltpu.VMEM((n,) + small.shape, F32) for n in (2, ny, nz, nx)]
        + [
            pltpu.SemaphoreType.DMA((2 * peers,)),
            pltpu.SemaphoreType.DMA((2 * peers,)),
            pltpu.SemaphoreType.DMA((peers,)),
            pltpu.SemaphoreType.DMA((peers,)),
        ],
        compiler_params=params(collective_id=0, has_side_effects=True),
        name="reduce_all",
    )(grads, small)


def route_slots(rank_row, point_count, total, row_count, shard_count, send_size, offset):
    slot_total = rank_row.shape[0]
    index = jnp.arange(slot_total, dtype=jnp.int32)
    live_slot = index < point_count
    moved = rank_row % total
    target_shard = jnp.where(live_slot, moved // row_count, shard_count)
    matches = target_shard[:, None] == jnp.arange(shard_count, dtype=jnp.int32)[None, :]
    earlier = (index[:, None] > index[None, :]).astype(BF16)
    before = jnp.dot(earlier, matches.astype(BF16), preferred_element_type=F32)
    ordinal = jnp.sum(jnp.where(matches, before, 0.0), axis=1).astype(jnp.int32)
    target = jnp.where(live_slot, target_shard * send_size + ordinal, shard_count * send_size)
    return target, (moved % row_count - offset) % row_count


def on_device(
    sizes, points, counts, hilbert_rank, patch_shift, norm_gain, project_in, project_out, cotangent
):
    shard_count = lax.axis_size("pts")
    row_count = cotangent.shape[1]
    width = points.shape[2]
    slot_total = points.shape[1]
    slot_size = slot_total // shard_count
    total = row_count * shard_count
    offset = patch_shift[0]
    limit = row_count - offset
    own_row = jnp.arange(row_count, dtype=jnp.int32)[:, None] < limit

    cot_rows = cotangent[0]
    cot_rolled = lax.dynamic_slice_in_dim(
        jnp.concatenate([cot_rows, cot_rows], axis=0), offset, row_count, 0
    )
    cot_next = shifted(cot_rolled, "pts", -1)

    target, position = route_slots(
        hilbert_rank[0], counts[0, 0], total, row_count, shard_count, slot_size, offset
    )
    slot = jnp.arange(slot_total, dtype=jnp.int32)
    out_position = jnp.max(
        jnp.where(target[:, None] == slot[None, :], position[:, None], -1), axis=0
    )
    outgoing = place(target, points[0], slot_total)
    in_position = lax.all_to_all(
        out_position.reshape(shard_count, slot_size), "pts", split_axis=0, concat_axis=0, tiled=True
    ).reshape(slot_total)
    incoming = lax.all_to_all(
        outgoing.reshape(shard_count, slot_size, width), "pts", split_axis=0, concat_axis=0, tiled=True
    ).reshape(slot_total, width)

    cot_window = jnp.where(own_row, cot_rolled, cot_next)
    grad_mixed = jnp.dot(cot_window, project_out.T, preferred_element_type=F32).astype(BF16)

    rolled = place(in_position, incoming, row_count)
    rolled_next = shifted(rolled, "pts", -1)
    window, normed, qkv = project(limit.reshape(1), rolled, rolled_next, norm_gain, project_in)
    mixed, d_qkv = attend(qkv, grad_mixed)
    grad_window, scale = input_grad(d_qkv, project_in, window, cot_window, norm_gain)
    grad_back = shifted(grad_window, "pts", 1)

    partial = weight_grad(normed, d_qkv, mixed, cot_window)
    block_window = (
        window.astype(F32) + jnp.dot(mixed, project_out, preferred_element_type=F32)
    ).astype(BF16)

    grad_rolled = jnp.where(own_row, grad_window, grad_back)
    returning = fetch(in_position, grad_rolled)
    returning, partial, scale, block_window = lax.optimization_barrier(
        (returning, partial, scale, block_window)
    )
    arrived = lax.all_to_all(
        returning.reshape(shard_count, slot_size, width), "pts", split_axis=0, concat_axis=0, tiled=True
    ).reshape(slot_total, width)
    block_back = shifted(block_window, "pts", 1)

    small = jnp.zeros((8, 128), F32).at[: width // 128].set(scale.reshape(width // 128, 128))
    summed, small = reduce_all(partial, small, sizes)

    block_rolled = jnp.where(own_row, block_window, block_back)
    block_rows = lax.dynamic_slice_in_dim(
        jnp.concatenate([block_rolled, block_rolled], axis=0), limit, row_count, 0
    )
    grad_points = fetch(target, arrived)
    factor = 1.0 / math.sqrt(total * lax.axis_size("rep"))
    return (
        block_rows[None],
        grad_points[None],
        summed[:, : 3 * width].astype(F32) * factor,
        summed[:, 3 * width :].astype(F32) * factor,
        small[: width // 128].reshape(width) * factor,
    )


def solution(mesh):
    spread = mesh.shape["pts"]
    sizes = {64: (4, 4, 8), 8: (2, 2, 2)}[spread]
    return jax.shard_map(
        functools.partial(on_device, sizes),
        mesh=mesh,
        in_specs=(
            P("rep", "pts", None),
            P("rep", "pts"),
            P("rep", "pts"),
            P("rep"),
            P(),
            P(),
            P(),
            P("rep", "pts", None),
        ),
        out_specs=(P("rep", "pts", None), P("rep", "pts", None), P(), P(), P()),
        check_vma=False,
    )
```

```python
import functools
import math

import jax
import jax.numpy as jnp
from jax import lax
from jax.experimental import pallas as pl
from jax.experimental.pallas import tpu as pltpu
from jax.sharding import PartitionSpec as P


HEAD_DIM = 64
EPSILON = 1e-05
MESH = pl.DeviceIdType.MESH
BF16 = jnp.bfloat16
F32 = jnp.float32
NT = (((1,), (1,)), ((), ()))
TN = (((0,), (0,)), ((), ()))


def params(**kw):
    return pltpu.CompilerParams(vmem_limit_bytes=56 << 20, **kw)


def shifted(value, axis, steps):
    count = lax.axis_size(axis)
    pairs = [(source, (source + steps) % count) for source in range(count)]
    return lax.ppermute(value, axis, pairs)


def place_kernel(dest_ref, src_ref, out_ref):
    block, depth = out_ref.shape[0], src_ref.shape[0]
    row = lax.broadcasted_iota(jnp.int32, (block, depth), 0) + pl.program_id(0) * block
    hot = jnp.where(row == dest_ref[...], 1.0, 0.0).astype(BF16)
    out_ref[...] = jnp.dot(hot, src_ref[...], preferred_element_type=F32).astype(BF16)


def place(dest, src, rows, block=512):
    depth, width = src.shape
    return pl.pallas_call(
        place_kernel,
        grid=(rows // block,),
        in_specs=[
            pl.BlockSpec((1, depth), lambda i: (0, 0)),
            pl.BlockSpec((depth, width), lambda i: (0, 0)),
        ],
        out_specs=pl.BlockSpec((block, width), lambda i: (i, 0)),
        out_shape=jax.ShapeDtypeStruct((rows, width), BF16),
        compiler_params=params(),
        name="place",
    )(dest.reshape(1, depth), src)


def fetch_kernel(index_ref, src_ref, out_ref):
    block, depth = out_ref.shape[0], src_ref.shape[0]
    column = lax.broadcasted_iota(jnp.int32, (block, depth), 1)
    hot = jnp.where(column == index_ref[...], 1.0, 0.0).astype(BF16)
    out_ref[...] = jnp.dot(hot, src_ref[...], preferred_element_type=F32).astype(BF16)


def fetch(index, src, block=512):
    depth, width = src.shape
    rows = index.shape[0]
    return pl.pallas_call(
        fetch_kernel,
        grid=(rows // block,),
        in_specs=[
            pl.BlockSpec((block, 1), lambda i: (i, 0)),
            pl.BlockSpec((depth, width), lambda i: (0, 0)),
        ],
        out_specs=pl.BlockSpec((block, width), lambda i: (i, 0)),
        out_shape=jax.ShapeDtypeStruct((rows, width), BF16),
        compiler_params=params(),
        name="fetch",
    )(index.reshape(rows, 1), src)


def unit_of(values):
    centre = jnp.mean(values, axis=-1, keepdims=True)
    deviation = values - centre
    inverse = lax.rsqrt(jnp.mean(deviation * deviation, axis=-1, keepdims=True) + EPSILON)
    return deviation * inverse, inverse


def project_kernel(limit_ref, own_ref, next_ref, gain_ref, weight_ref, win_ref, normed_ref, qkv_ref):
    block = own_ref.shape[0]
    row = lax.broadcasted_iota(jnp.int32, own_ref.shape, 0) + pl.program_id(0) * block
    values = jnp.where(
        row < limit_ref[0], own_ref[...].astype(F32), next_ref[...].astype(F32)
    )
    unit, _ = unit_of(values)
    normed = (unit * gain_ref[...]).astype(BF16)
    win_ref[...] = values.astype(BF16)
    normed_ref[...] = normed
    qkv_ref[...] = jnp.dot(normed, weight_ref[...], preferred_element_type=F32).astype(BF16)


def project(limit, own, following, gain, weight, block=512):
    rows, width = own.shape
    wide = weight.shape[1]
    tile = pl.BlockSpec((block, width), lambda i: (i, 0))
    return pl.pallas_call(
        project_kernel,
        grid=(rows // block,),
        in_specs=[
            pl.BlockSpec(memory_space=pltpu.SMEM),
            tile,
            tile,
            pl.BlockSpec((1, width), lambda i: (0, 0)),
            pl.BlockSpec((width, wide), lambda i: (0, 0)),
        ],
        out_specs=[tile, tile, pl.BlockSpec((block, wide), lambda i: (i, 0))],
        out_shape=[
            jax.ShapeDtypeStruct((rows, width), BF16),
            jax.ShapeDtypeStruct((rows, width), BF16),
            jax.ShapeDtypeStruct((rows, wide), BF16),
        ],
        compiler_params=params(),
        name="project",
    )(limit, own, following, gain.reshape(1, width), weight)


def attend_kernel(q_ref, k_ref, v_ref, g_ref, mixed_ref, d_ref, dk_ref, dv_ref, *, chunk):
    rows = q_ref.shape[0]
    keys, values = k_ref[...], v_ref[...]
    lane = lax.broadcasted_iota(jnp.int32, (1, 128), 1)
    line = lax.broadcasted_iota(jnp.int32, (128, 1), 0)
    lanes = [jnp.where(lane < HEAD_DIM, 1.0, 0.0), jnp.where(lane < HEAD_DIM, 0.0, 1.0)]
    lines = [jnp.where(line < HEAD_DIM, 1.0, 0.0), jnp.where(line < HEAD_DIM, 0.0, 1.0)]
    keys_t = keys.astype(F32).T
    values_t = values.astype(F32).T
    keys_t = [(keys_t * m).astype(BF16) for m in lines]
    values_t = [(values_t * m).astype(BF16) for m in lines]
    steps = rows // chunk
    for at in range(steps):
        window = slice(at * chunk, (at + 1) * chunk)
        q_all = q_ref[window, :].astype(F32) * HEAD_DIM ** (-0.5)
        g_all = g_ref[window, :].astype(F32)
        q = jnp.concatenate([(q_all * m).astype(BF16) for m in lanes], axis=0)
        g = jnp.concatenate([(g_all * m).astype(BF16) for m in lanes], axis=0)
        logits = lax.dot_general(keys, q, NT, preferred_element_type=F32)
        power = jnp.exp(logits - jnp.max(logits, axis=0, keepdims=True))
        share = power * (1.0 / jnp.sum(power, axis=0, keepdims=True))
        share_b = share.astype(BF16)
        dshare = lax.dot_general(values, g, NT, preferred_element_type=F32)
        dot = jnp.sum(dshare * share, axis=0, keepdims=True)
        dlogits = (share * (dshare - dot)).astype(BF16)
        mixed_t = jnp.zeros((128, chunk), F32)
        dq_t = jnp.zeros((128, chunk), F32)
        for head in range(2):
            part = slice(head * chunk, (head + 1) * chunk)
            mixed_t += jnp.dot(values_t[head], share_b[:, part], preferred_element_type=F32)
            dq_t += jnp.dot(keys_t[head], dlogits[:, part], preferred_element_type=F32)
        dv = jnp.dot(share_b, g, preferred_element_type=F32)
        dk = jnp.dot(dlogits, q, preferred_element_type=F32)
        if at > 0:
            dv += dv_ref[...]
            dk += dk_ref[...]
        if at < steps - 1:
            dv_ref[...] = dv
            dk_ref[...] = dk
        else:
            d_ref[1] = dk.astype(BF16)
            d_ref[2] = dv.astype(BF16)
        mixed_ref[window, :] = mixed_t.T.astype(BF16)
        d_ref[0, window, :] = (dq_t * HEAD_DIM ** (-0.5)).T.astype(BF16)


def attend(qkv, grads, chunk=512):
    rows, width = grads.shape
    pairs = width // 128
    return pl.pallas_call(
        functools.partial(attend_kernel, chunk=chunk),
        grid=(pairs,),
        in_specs=[
            pl.BlockSpec((rows, 128), lambda j: (0, j)),
            pl.BlockSpec((rows, 128), lambda j: (0, pairs + j)),
            pl.BlockSpec((rows, 128), lambda j: (0, 2 * pairs + j)),
            pl.BlockSpec((rows, 128), lambda j: (0, j)),
        ],
        out_specs=[
            pl.BlockSpec((rows, 128), lambda j: (0, j)),
            pl.BlockSpec((3, rows, 128), lambda j: (0, 0, j)),
        ],
        out_shape=[
            jax.ShapeDtypeStruct((rows, width), BF16),
            jax.ShapeDtypeStruct((3, rows, width), BF16),
        ],
        scratch_shapes=[pltpu.VMEM((rows, 128), F32), pltpu.VMEM((rows, 128), F32)],
        compiler_params=params(),
        name="attend",
    )(qkv, qkv, qkv, grads)


def input_grad_kernel(d_ref, weight_ref, win_ref, cot_ref, gain_ref, out_ref, scale_ref):
    width = win_ref.shape[1]
    grad = jnp.zeros(win_ref.shape, F32)
    for part in range(3):
        grad += lax.dot_general(
            d_ref[part],
            weight_ref[:, part * width : (part + 1) * width],
            NT,
            preferred_element_type=F32,
        )
    unit, inverse = unit_of(win_ref[...].astype(F32))
    product = grad * unit

    @pl.when(pl.program_id(0) == 0)
    def _():
        scale_ref[...] = jnp.zeros_like(scale_ref)

    scale_ref[...] += jnp.sum(product, axis=0, keepdims=True)
    weighted = grad * gain_ref[...]
    branch = inverse * (
        weighted
        - jnp.mean(weighted, axis=-1, keepdims=True)
        - unit * jnp.mean(product * gain_ref[...], axis=-1, keepdims=True)
    )
    out_ref[...] = (cot_ref[...].astype(F32) + branch).astype(BF16)


def input_grad(d, weight, win, cot, gain, block=512):
    rows, width = win.shape
    tile = pl.BlockSpec((block, width), lambda i: (i, 0))
    return pl.pallas_call(
        input_grad_kernel,
        grid=(rows // block,),
        in_specs=[
            pl.BlockSpec((3, block, width), lambda i: (0, i, 0)),
            pl.BlockSpec(weight.shape, lambda i: (0, 0)),
            tile,
            tile,
            pl.BlockSpec((1, width), lambda i: (0, 0)),
        ],
        out_specs=[tile, pl.BlockSpec((1, width), lambda i: (0, 0))],
        out_shape=[
            jax.ShapeDtypeStruct((rows, width), BF16),
            jax.ShapeDtypeStruct((1, width), F32),
        ],
        compiler_params=params(),
        name="input_grad",
    )(d, weight, win, cot, gain.reshape(1, width))


def weight_grad_kernel(half_ref, normed_ref, d_ref, mixed_ref, cot_ref, out_ref):
    part = half_ref[0] * 2 + pl.program_id(0)
    middle = out_ref.shape[2]

    def emit(left, right):
        grad = lax.dot_general(left, right, TN, preferred_element_type=F32).astype(BF16)
        out_ref[0] = grad[:, :middle]
        out_ref[1] = grad[:, middle:]

    @pl.when(part < 3)
    def _():
        emit(normed_ref[...], d_ref[0])

    @pl.when(part == 3)
    def _():
        emit(mixed_ref[...], cot_ref[...])


def weight_grad(half, normed, d, mixed, cot):
    rows, width = normed.shape
    whole = pl.BlockSpec((rows, width), lambda j, half: (0, 0))
    return pl.pallas_call(
        weight_grad_kernel,
        grid_spec=pltpu.PrefetchScalarGridSpec(
            num_scalar_prefetch=1,
            grid=(2,),
            in_specs=[
                whole,
                pl.BlockSpec(
                    (1, rows, width), lambda j, half: (jnp.minimum(half[0] * 2 + j, 2), 0, 0)
                ),
                whole,
                whole,
            ],
            out_specs=pl.BlockSpec((2, width, width // 2), lambda j, half: (j, 0, 0)),
        ),
        out_shape=jax.ShapeDtypeStruct((4, width, width // 2), BF16),
        compiler_params=params(),
        name="weight_grad",
    )(half.reshape(1), normed, d, mixed, cot)


def reduce_kernel(
    sizes, q_ref, s_ref, out_ref, t_ref,
    band, in_z, in_x, small, small_core, small_y, small_z, small_x,
    send_sem, recv_sem, small_send, small_recv,
):
    nx, ny, nz = sizes
    rows, part_w = q_ref.shape
    half_w = part_w * ny
    band_h, piece_h = rows // nz, rows // nz // nx
    me = lax.axis_index("pts")
    y = lax.axis_index("rep")
    core = lax.rem(me, 2)
    z = lax.rem(me // 2, nz)
    x = me // (2 * nz)

    def at(x_, y_, z_, core_):
        return {"pts": (x_ * nz + z_) * 2 + core_, "rep": y_}

    by_core = [(at(x, y, z, 1 - core), 1 - core)]
    by_y = [(at(x, lax.rem(y + k, ny), z, core), lax.rem(y + k, ny)) for k in range(1, ny)]
    by_z = [(at(x, y, lax.rem(z + k, nz), core), lax.rem(z + k, nz)) for k in range(1, nz)]
    by_x = [(at(lax.rem(x + k, nx), y, z, core), lax.rem(x + k, nx)) for k in range(1, nx)]
    everyone = by_core + by_y + by_z + by_x
    barrier = pltpu.get_barrier_semaphore()
    for device, _ in everyone:
        pl.semaphore_signal(barrier, inc=1, device_id=device, device_id_type=MESH)
    pl.semaphore_wait(barrier, len(everyone))

    used = [0]
    small_used = [0]

    def send(src, dst, device):
        slot = used[0]
        used[0] += 1
        copy = pltpu.make_async_remote_copy(
            src_ref=src, dst_ref=dst, send_sem=send_sem.at[slot], recv_sem=recv_sem.at[slot],
            device_id=device, device_id_type=MESH,
        )
        copy.start()
        return copy

    def send_small(peers, slots, mine):
        slots[mine] = small[...]
        copies = []
        for device, _ in peers:
            slot = small_used[0]
            small_used[0] += 1
            copy = pltpu.make_async_remote_copy(
                src_ref=small, dst_ref=slots.at[mine],
                send_sem=small_send.at[slot], recv_sem=small_recv.at[slot],
                device_id=device, device_id_type=MESH,
            )
            copy.start()
            copies.append(copy)
        return copies

    def add_small(copies, slots):
        for copy in copies:
            copy.wait()
        total = slots[0]
        for k in range(1, slots.shape[0]):
            total += slots[k]
        small[...] = total

    def columns(index, width):
        return pl.ds(pl.multiple_of(index * width, width), width)

    def lines(index, height):
        return pl.ds(pl.multiple_of(index * height, height), height)

    small[...] = s_ref[...]
    copies = [
        send(q_ref.at[lines(i, band_h), :], in_z.at[k], device) for k, (device, i) in enumerate(by_z)
    ]
    small_copies = send_small(by_z, small_z, z)
    for copy in copies:
        copy.wait()
    total = q_ref[lines(z, band_h), :].astype(F32)
    for k in range(nz - 1):
        total += in_z[k].astype(F32)
    band[...] = total.astype(BF16)
    copies = [
        send(band.at[lines(i, piece_h), :], in_x.at[k], device) for k, (device, i) in enumerate(by_x)
    ]
    add_small(small_copies, small_z)
    small_copies = send_small(by_x, small_x, x)
    for copy in copies:
        copy.wait()
    total = band[lines(x, piece_h), :].astype(F32)
    for k in range(nx - 1):
        total += in_x[k].astype(F32)

    column = columns(core * ny + y, part_w)
    first = pl.multiple_of(z * band_h + x * piece_h, piece_h)
    out_ref[pl.ds(first, piece_h), column] = total.astype(BF16)

    def spread(peers, view):
        return [send(view, view, device) for device, _ in peers]

    copies = spread(by_x, out_ref.at[pl.ds(first, piece_h), column])
    add_small(small_copies, small_x)
    small_copies = send_small(by_y, small_y, y)
    for copy in copies:
        copy.wait()
    copies = spread(by_z, out_ref.at[lines(z, band_h), column])
    add_small(small_copies, small_y)
    small_copies = send_small(by_core, small_core, core)
    for copy in copies:
        copy.wait()
    own = out_ref.at[:, column]
    if ny == 4:
        turn = 1 - 2 * core
        ahead = at(x, lax.rem(y + turn + ny, ny), z, core)
        behind = at(x, lax.rem(y - turn + ny, ny), z, core)
        forth, back = send(own, own, ahead), send(own, own, behind)
        forth.wait()
        came = out_ref.at[:, columns(core * ny + lax.rem(y - turn + ny, ny), part_w)]
        passed = send(came, came, ahead)
        add_small(small_copies, small_core)
        back.wait()
        passed.wait()
    else:
        copies = spread(by_y, own)
        add_small(small_copies, small_core)
        for copy in copies:
            copy.wait()
    t_ref[...] = small[...]
    for copy in spread(by_core, out_ref.at[:, columns(core, half_w)]):
        copy.wait()


def reduce_all(quarter, small, sizes):
    nx, ny, nz = sizes
    rows, part = quarter.shape
    peers = 1 + (ny - 1) + (nz - 1) + (nx - 1)
    vmem = pl.BlockSpec(memory_space=pltpu.VMEM)
    buffers = [
        (rows // nz, part), (nz - 1, rows // nz, part), (max(nx - 1, 1), rows // nz // nx, part),
    ]
    return pl.pallas_call(
        functools.partial(reduce_kernel, sizes),
        in_specs=[vmem, vmem],
        out_specs=[vmem, vmem],
        out_shape=[
            jax.ShapeDtypeStruct((rows, part * ny * 2), BF16),
            jax.ShapeDtypeStruct(small.shape, F32),
        ],
        scratch_shapes=[pltpu.VMEM(shape, BF16) for shape in buffers]
        + [pltpu.VMEM(small.shape, F32)]
        + [pltpu.VMEM((n,) + small.shape, F32) for n in (2, ny, nz, nx)]
        + [
            pltpu.SemaphoreType.DMA((2 * peers,)),
            pltpu.SemaphoreType.DMA((2 * peers,)),
            pltpu.SemaphoreType.DMA((peers,)),
            pltpu.SemaphoreType.DMA((peers,)),
        ],
        compiler_params=params(collective_id=0, has_side_effects=True),
        name="reduce_all",
    )(quarter, small)


def scatter_core(normed, d, mixed, cot):
    pts = lax.axis_size("pts")
    core = lax.rem(lax.axis_index("pts"), 2)
    swap = [(source, source ^ 1) for source in range(pts)]
    theirs = lax.ppermute(weight_grad(1 - core, normed, d, mixed, cot), "pts", swap)
    return (
        weight_grad(core, normed, d, mixed, cot).astype(F32) + theirs.astype(F32)
    ).astype(BF16)


def scatter_rep(half):
    reps = lax.axis_size("rep")
    y = lax.axis_index("rep")

    def piece(step):
        return lax.dynamic_index_in_dim(half, lax.rem(y + step, reps), 0, keepdims=False)

    total = piece(0).astype(F32)
    for step in range(1, reps):
        total += shifted(piece(step), "rep", step).astype(F32)
    return total.astype(BF16)


def route_slots(rank_row, point_count, total, row_count, shard_count, send_size, offset):
    slot_total = rank_row.shape[0]
    index = jnp.arange(slot_total, dtype=jnp.int32)
    live_slot = index < point_count
    moved = rank_row % total
    target_shard = jnp.where(live_slot, moved // row_count, shard_count)
    matches = target_shard[:, None] == jnp.arange(shard_count, dtype=jnp.int32)[None, :]
    earlier = (index[:, None] > index[None, :]).astype(BF16)
    before = jnp.dot(earlier, matches.astype(BF16), preferred_element_type=F32)
    ordinal = jnp.sum(jnp.where(matches, before, 0.0), axis=1).astype(jnp.int32)
    target = jnp.where(live_slot, target_shard * send_size + ordinal, shard_count * send_size)
    return target, (moved % row_count - offset) % row_count


def on_device(
    sizes, points, counts, hilbert_rank, patch_shift, norm_gain, project_in, project_out, cotangent
):
    shard_count = lax.axis_size("pts")
    row_count = cotangent.shape[1]
    width = points.shape[2]
    slot_total = points.shape[1]
    slot_size = slot_total // shard_count
    total = row_count * shard_count
    offset = patch_shift[0]
    limit = row_count - offset
    own_row = jnp.arange(row_count, dtype=jnp.int32)[:, None] < limit

    cot_rows = cotangent[0]
    cot_next = shifted(cot_rows, "pts", -1)

    target, position = route_slots(
        hilbert_rank[0], counts[0, 0], total, row_count, shard_count, slot_size, offset
    )
    slot = jnp.arange(slot_total, dtype=jnp.int32)
    out_position = jnp.max(
        jnp.where(target[:, None] == slot[None, :], position[:, None], -1), axis=0
    )
    outgoing = place(target, points[0], slot_total)
    outgoing, cot_next = lax.optimization_barrier((outgoing, cot_next))
    in_position = lax.all_to_all(
        out_position.reshape(shard_count, slot_size), "pts", split_axis=0, concat_axis=0, tiled=True
    ).reshape(slot_total)
    incoming = lax.all_to_all(
        outgoing.reshape(shard_count, slot_size, width), "pts", split_axis=0, concat_axis=0, tiled=True
    ).reshape(slot_total, width)

    cot_window = lax.dynamic_slice_in_dim(
        jnp.concatenate([cot_rows, cot_next], axis=0), offset, row_count, 0
    )
    grad_mixed = jnp.dot(cot_window, project_out.T, preferred_element_type=F32).astype(BF16)

    rolled = place(in_position, incoming, row_count)
    rolled_next = shifted(rolled, "pts", -1)
    window, normed, qkv = project(limit.reshape(1), rolled, rolled_next, norm_gain, project_in)
    mixed, d_qkv = attend(qkv, grad_mixed)
    grad_window, scale = input_grad(d_qkv, project_in, window, cot_window, norm_gain)
    grad_back = shifted(grad_window, "pts", 1)

    half = scatter_core(normed, d_qkv, mixed, cot_window)
    grad_back, half = lax.optimization_barrier((grad_back, half))
    quarter = scatter_rep(half)
    block_window = (
        window.astype(F32) + jnp.dot(mixed, project_out, preferred_element_type=F32)
    ).astype(BF16)

    grad_rolled = jnp.where(own_row, grad_window, grad_back)
    returning = fetch(in_position, grad_rolled)
    quarter, scale, block_window, _ = lax.optimization_barrier(
        (quarter, scale, block_window, returning)
    )
    arrived = lax.all_to_all(
        returning.reshape(shard_count, slot_size, width), "pts", split_axis=0, concat_axis=0, tiled=True
    ).reshape(slot_total, width)
    block_back = shifted(block_window, "pts", 1)

    small = jnp.zeros((8, 128), F32).at[: width // 128].set(scale.reshape(width // 128, 128))
    summed, small = reduce_all(quarter, small, sizes)

    block_rows = lax.dynamic_slice_in_dim(
        jnp.concatenate([block_back, block_window], axis=0), limit, row_count, 0
    )
    grad_points = fetch(target, arrived)
    factor = 1.0 / math.sqrt(total * lax.axis_size("rep"))
    return (
        block_rows[None],
        grad_points[None],
        summed[:, : 3 * width].astype(F32) * factor,
        summed[:, 3 * width :].astype(F32) * factor,
        small[: width // 128].reshape(width) * factor,
    )


def solution(mesh):
    spread = mesh.shape["pts"]
    sizes = {64: (4, 4, 8), 8: (2, 2, 2), 4: (1, 4, 2)}[spread]
    return jax.shard_map(
        functools.partial(on_device, sizes),
        mesh=mesh,
        in_specs=(
            P("rep", "pts", None),
            P("rep", "pts"),
            P("rep", "pts"),
            P("rep"),
            P(),
            P(),
            P(),
            P("rep", "pts", None),
        ),
        out_specs=(P("rep", "pts", None), P("rep", "pts", None), P(), P(), P()),
        check_vma=False,
    )
```

```python
import functools
import math

import jax
import jax.numpy as jnp
from jax import lax
from jax.experimental import pallas as pl
from jax.experimental.pallas import tpu as pltpu
from jax.sharding import PartitionSpec as P


HEAD_DIM = 64
EPSILON = 1e-05
MESH = pl.DeviceIdType.MESH
BF16 = jnp.bfloat16
F32 = jnp.float32
NT = (((1,), (1,)), ((), ()))
TN = (((0,), (0,)), ((), ()))


def params(**kw):
    return pltpu.CompilerParams(vmem_limit_bytes=56 << 20, **kw)


def shifted(value, axis, steps):
    count = lax.axis_size(axis)
    pairs = [(source, (source + steps) % count) for source in range(count)]
    return lax.ppermute(value, axis, pairs)


def place_kernel(dest_ref, src_ref, out_ref):
    block, depth = out_ref.shape[0], src_ref.shape[0]
    row = lax.broadcasted_iota(jnp.int32, (block, depth), 0) + pl.program_id(0) * block
    hot = jnp.where(row == dest_ref[...], 1.0, 0.0).astype(BF16)
    out_ref[...] = jnp.dot(hot, src_ref[...], preferred_element_type=F32).astype(BF16)


def place(dest, src, rows, block=512):
    depth, width = src.shape
    return pl.pallas_call(
        place_kernel,
        grid=(rows // block,),
        in_specs=[
            pl.BlockSpec((1, depth), lambda i: (0, 0)),
            pl.BlockSpec((depth, width), lambda i: (0, 0)),
        ],
        out_specs=pl.BlockSpec((block, width), lambda i: (i, 0)),
        out_shape=jax.ShapeDtypeStruct((rows, width), BF16),
        compiler_params=params(),
        name="place",
    )(dest.reshape(1, depth), src)


def fetch_kernel(index_ref, src_ref, out_ref):
    block, depth = out_ref.shape[0], src_ref.shape[0]
    column = lax.broadcasted_iota(jnp.int32, (block, depth), 1)
    hot = jnp.where(column == index_ref[...], 1.0, 0.0).astype(BF16)
    out_ref[...] = jnp.dot(hot, src_ref[...], preferred_element_type=F32).astype(BF16)


def fetch(index, src, block=512):
    depth, width = src.shape
    rows = index.shape[0]
    assert index.shape == (rows, 1)
    return pl.pallas_call(
        fetch_kernel,
        grid=(rows // block,),
        in_specs=[
            pl.BlockSpec((block, 1), lambda i: (i, 0)),
            pl.BlockSpec((depth, width), lambda i: (0, 0)),
        ],
        out_specs=pl.BlockSpec((block, width), lambda i: (i, 0)),
        out_shape=jax.ShapeDtypeStruct((rows, width), BF16),
        compiler_params=params(),
        name="fetch",
    )(index, src)


def deliver_kernel(count, out_ref, pos_ref, in_ref, in_pos_ref, sems, own_sems):
    me = lax.axis_index("pts")
    barrier = pltpu.get_barrier_semaphore()

    def greet(k, carry):
        pl.semaphore_signal(
            barrier, inc=1, device_id={"pts": lax.rem(me + k, count)}, device_id_type=MESH
        )
        return carry

    lax.fori_loop(1, count, greet, 0)
    pl.semaphore_wait(barrier, count - 1)
    own = [
        pltpu.make_async_copy(pos_ref.at[me], in_pos_ref.at[me], own_sems.at[0]),
        pltpu.make_async_copy(out_ref.at[me], in_ref.at[me], own_sems.at[1]),
    ]
    for copy in own:
        copy.start()

    def copies(j):
        near = j // 2 + 1
        k = near + lax.rem(j, 2) * (count - 2 * near)
        peer = lax.rem(me + k, count)
        return [
            pltpu.make_async_remote_copy(
                src_ref=src.at[peer], dst_ref=dst.at[me],
                send_sem=sems.at[2 * row, k], recv_sem=sems.at[2 * row + 1, k],
                device_id={"pts": peer}, device_id_type=MESH,
            )
            for row, (src, dst) in enumerate(((pos_ref, in_pos_ref), (out_ref, in_ref)))
        ]

    def start(j, carry):
        for copy in copies(j):
            copy.start()
        return carry

    def finish(j, carry):
        for copy in copies(j):
            copy.wait()
        return carry

    lax.fori_loop(0, count - 1, start, 0)
    lax.fori_loop(0, count - 1, finish, 0)
    for copy in own:
        copy.wait()


def deliver(outgoing, position):
    count = outgoing.shape[0]
    anywhere = pl.BlockSpec(memory_space=pl.ANY)
    return pl.pallas_call(
        functools.partial(deliver_kernel, count),
        in_specs=[anywhere, anywhere],
        out_specs=[anywhere, anywhere],
        out_shape=[
            jax.ShapeDtypeStruct(outgoing.shape, outgoing.dtype),
            jax.ShapeDtypeStruct(position.shape, position.dtype),
        ],
        scratch_shapes=[pltpu.SemaphoreType.DMA((4, count)), pltpu.SemaphoreType.DMA((2,))],
        compiler_params=params(collective_id=1, has_side_effects=True),
        name="deliver",
    )(outgoing, position)


def unit_of(values):
    centre = jnp.mean(values, axis=-1, keepdims=True)
    deviation = values - centre
    inverse = lax.rsqrt(jnp.mean(deviation * deviation, axis=-1, keepdims=True) + EPSILON)
    return deviation * inverse, inverse


def project_kernel(limit_ref, own_ref, next_ref, gain_ref, weight_ref, win_ref, normed_ref, qkv_ref):
    block = own_ref.shape[0]
    row = lax.broadcasted_iota(jnp.int32, own_ref.shape, 0) + pl.program_id(0) * block
    values = jnp.where(
        row < limit_ref[0], own_ref[...].astype(F32), next_ref[...].astype(F32)
    )
    unit, _ = unit_of(values)
    normed = (unit * gain_ref[...]).astype(BF16)
    win_ref[...] = values.astype(BF16)
    normed_ref[...] = normed
    qkv_ref[...] = jnp.dot(normed, weight_ref[...], preferred_element_type=F32).astype(BF16)


def project(limit, own, following, gain, weight, block=512):
    rows, width = own.shape
    wide = weight.shape[1]
    tile = pl.BlockSpec((block, width), lambda i: (i, 0))
    return pl.pallas_call(
        project_kernel,
        grid=(rows // block,),
        in_specs=[
            pl.BlockSpec(memory_space=pltpu.SMEM),
            tile,
            tile,
            pl.BlockSpec((1, width), lambda i: (0, 0)),
            pl.BlockSpec((width, wide), lambda i: (0, 0)),
        ],
        out_specs=[tile, tile, pl.BlockSpec((block, wide), lambda i: (i, 0))],
        out_shape=[
            jax.ShapeDtypeStruct((rows, width), BF16),
            jax.ShapeDtypeStruct((rows, width), BF16),
            jax.ShapeDtypeStruct((rows, wide), BF16),
        ],
        compiler_params=params(),
        name="project",
    )(limit, own, following, gain.reshape(1, width), weight)


def attend_kernel(q_ref, k_ref, v_ref, g_ref, mixed_ref, d_ref, dk_ref, dv_ref, *, chunk):
    rows = q_ref.shape[0]
    keys, values = k_ref[...], v_ref[...]
    lane = lax.broadcasted_iota(jnp.int32, (1, 128), 1)
    line = lax.broadcasted_iota(jnp.int32, (128, 1), 0)
    lanes = [jnp.where(lane < HEAD_DIM, 1.0, 0.0), jnp.where(lane < HEAD_DIM, 0.0, 1.0)]
    lines = [jnp.where(line < HEAD_DIM, 1.0, 0.0), jnp.where(line < HEAD_DIM, 0.0, 1.0)]
    keys_t = keys.astype(F32).T
    values_t = values.astype(F32).T
    keys_t = [(keys_t * m).astype(BF16) for m in lines]
    values_t = [(values_t * m).astype(BF16) for m in lines]
    steps = rows // chunk
    for at in range(steps):
        window = slice(at * chunk, (at + 1) * chunk)
        q_all = q_ref[window, :].astype(F32) * HEAD_DIM ** (-0.5)
        g_all = g_ref[window, :].astype(F32)
        q = jnp.concatenate([(q_all * m).astype(BF16) for m in lanes], axis=0)
        g = jnp.concatenate([(g_all * m).astype(BF16) for m in lanes], axis=0)
        logits = lax.dot_general(keys, q, NT, preferred_element_type=F32)
        power = jnp.exp(logits - jnp.max(logits, axis=0, keepdims=True))
        share = power * (1.0 / jnp.sum(power, axis=0, keepdims=True))
        share_b = share.astype(BF16)
        dshare = lax.dot_general(values, g, NT, preferred_element_type=F32)
        dot = jnp.sum(dshare * share, axis=0, keepdims=True)
        dlogits = (share * (dshare - dot)).astype(BF16)
        mixed_t = jnp.zeros((128, chunk), F32)
        dq_t = jnp.zeros((128, chunk), F32)
        for head in range(2):
            part = slice(head * chunk, (head + 1) * chunk)
            mixed_t += jnp.dot(values_t[head], share_b[:, part], preferred_element_type=F32)
            dq_t += jnp.dot(keys_t[head], dlogits[:, part], preferred_element_type=F32)
        dv = jnp.dot(share_b, g, preferred_element_type=F32)
        dk = jnp.dot(dlogits, q, preferred_element_type=F32)
        if at > 0:
            dv += dv_ref[...]
            dk += dk_ref[...]
        if at < steps - 1:
            dv_ref[...] = dv
            dk_ref[...] = dk
        else:
            d_ref[1] = dk.astype(BF16)
            d_ref[2] = dv.astype(BF16)
        mixed_ref[window, :] = mixed_t.T.astype(BF16)
        d_ref[0, window, :] = (dq_t * HEAD_DIM ** (-0.5)).T.astype(BF16)


def attend(qkv, grads, chunk=512):
    rows, width = grads.shape
    pairs = width // 128
    return pl.pallas_call(
        functools.partial(attend_kernel, chunk=chunk),
        grid=(pairs,),
        in_specs=[
            pl.BlockSpec((rows, 128), lambda j: (0, j)),
            pl.BlockSpec((rows, 128), lambda j: (0, pairs + j)),
            pl.BlockSpec((rows, 128), lambda j: (0, 2 * pairs + j)),
            pl.BlockSpec((rows, 128), lambda j: (0, j)),
        ],
        out_specs=[
            pl.BlockSpec((rows, 128), lambda j: (0, j)),
            pl.BlockSpec((3, rows, 128), lambda j: (0, 0, j)),
        ],
        out_shape=[
            jax.ShapeDtypeStruct((rows, width), BF16),
            jax.ShapeDtypeStruct((3, rows, width), BF16),
        ],
        scratch_shapes=[pltpu.VMEM((rows, 128), F32), pltpu.VMEM((rows, 128), F32)],
        compiler_params=params(),
        name="attend",
    )(qkv, qkv, qkv, grads)


def input_grad_kernel(d_ref, weight_ref, win_ref, cot_ref, gain_ref, out_ref, scale_ref):
    width = win_ref.shape[1]
    grad = jnp.zeros(win_ref.shape, F32)
    for part in range(3):
        grad += lax.dot_general(
            d_ref[part],
            weight_ref[:, part * width : (part + 1) * width],
            NT,
            preferred_element_type=F32,
        )
    unit, inverse = unit_of(win_ref[...].astype(F32))
    product = grad * unit

    @pl.when(pl.program_id(0) == 0)
    def _():
        scale_ref[...] = jnp.zeros_like(scale_ref)

    scale_ref[...] += jnp.sum(product, axis=0, keepdims=True)
    weighted = grad * gain_ref[...]
    branch = inverse * (
        weighted
        - jnp.mean(weighted, axis=-1, keepdims=True)
        - unit * jnp.mean(product * gain_ref[...], axis=-1, keepdims=True)
    )
    out_ref[...] = (cot_ref[...].astype(F32) + branch).astype(BF16)


def input_grad(d, weight, win, cot, gain, block=512):
    rows, width = win.shape
    tile = pl.BlockSpec((block, width), lambda i: (i, 0))
    return pl.pallas_call(
        input_grad_kernel,
        grid=(rows // block,),
        in_specs=[
            pl.BlockSpec((3, block, width), lambda i: (0, i, 0)),
            pl.BlockSpec(weight.shape, lambda i: (0, 0)),
            tile,
            tile,
            pl.BlockSpec((1, width), lambda i: (0, 0)),
        ],
        out_specs=[tile, pl.BlockSpec((1, width), lambda i: (0, 0))],
        out_shape=[
            jax.ShapeDtypeStruct((rows, width), BF16),
            jax.ShapeDtypeStruct((1, width), F32),
        ],
        compiler_params=params(),
        name="input_grad",
    )(d, weight, win, cot, gain.reshape(1, width))


def weight_grad_kernel(half_ref, normed_ref, d_ref, mixed_ref, cot_ref, out_ref):
    part = half_ref[0] * 2 + pl.program_id(0)
    middle = out_ref.shape[2]

    def emit(left, right):
        grad = lax.dot_general(left, right, TN, preferred_element_type=F32).astype(BF16)
        out_ref[0] = grad[:, :middle]
        out_ref[1] = grad[:, middle:]

    @pl.when(part < 3)
    def _():
        emit(normed_ref[...], d_ref[0])

    @pl.when(part == 3)
    def _():
        emit(mixed_ref[...], cot_ref[...])


def weight_grad(half, normed, d, mixed, cot):
    rows, width = normed.shape
    whole = pl.BlockSpec((rows, width), lambda j, half: (0, 0))
    return pl.pallas_call(
        weight_grad_kernel,
        grid_spec=pltpu.PrefetchScalarGridSpec(
            num_scalar_prefetch=1,
            grid=(2,),
            in_specs=[
                whole,
                pl.BlockSpec(
                    (1, rows, width), lambda j, half: (jnp.minimum(half[0] * 2 + j, 2), 0, 0)
                ),
                whole,
                whole,
            ],
            out_specs=pl.BlockSpec((2, width, width // 2), lambda j, half: (j, 0, 0)),
        ),
        out_shape=jax.ShapeDtypeStruct((4, width, width // 2), BF16),
        compiler_params=params(),
        name="weight_grad",
    )(half.reshape(1), normed, d, mixed, cot)


def return_kernel(
    sizes, count, q_ref, s_ref, back_ref, out_ref, t_ref, arrived_ref,
    band, in_z, in_x, small, small_core, small_y, small_z, small_x,
    send_sem, recv_sem, small_send, small_recv, slot_sems, own_sem,
):
    nx, ny, nz = sizes
    rows, part_w = q_ref.shape
    half_w = part_w * ny
    band_h, piece_h = rows // nz, rows // nz // nx
    me = lax.axis_index("pts")
    y = lax.axis_index("rep")
    core = lax.rem(me, 2)
    z = lax.rem(me // 2, nz)
    x = me // (2 * nz)

    def at(x_, y_, z_, core_):
        return {"pts": (x_ * nz + z_) * 2 + core_, "rep": y_}

    by_core = [(at(x, y, z, 1 - core), 1 - core)]
    by_y = [(at(x, lax.rem(y + k, ny), z, core), lax.rem(y + k, ny)) for k in range(1, ny)]
    by_z = [(at(x, y, lax.rem(z + k, nz), core), lax.rem(z + k, nz)) for k in range(1, nz)]
    by_x = [(at(lax.rem(x + k, nx), y, z, core), lax.rem(x + k, nx)) for k in range(1, nx)]
    barrier = pltpu.get_barrier_semaphore()

    def greet(k, carry):
        pl.semaphore_signal(
            barrier, inc=1, device_id={"pts": lax.rem(me + k, count)}, device_id_type=MESH
        )
        return carry

    lax.fori_loop(1, count, greet, 0)
    for device, _ in by_y:
        pl.semaphore_signal(barrier, inc=1, device_id=device, device_id_type=MESH)
    pl.semaphore_wait(barrier, count - 1 + len(by_y))

    def slot_copy(j):
        near = j // 2 + 1
        k = near + lax.rem(j, 2) * (count - 2 * near)
        peer = lax.rem(me + k, count)
        return pltpu.make_async_remote_copy(
            src_ref=back_ref.at[peer], dst_ref=arrived_ref.at[me],
            send_sem=slot_sems.at[0, k], recv_sem=slot_sems.at[1, k],
            device_id={"pts": peer}, device_id_type=MESH,
        )

    batches = 9
    edges = [(count - 1) * b // batches for b in range(batches + 1)]

    def start_slot(j, carry):
        slot_copy(j).start()
        return carry

    def sent_slot(j, carry):
        slot_copy(j).wait_send()
        return carry

    def came_slot(j, carry):
        slot_copy(j).wait_recv()
        return carry

    def issue(b):
        lax.fori_loop(edges[b], edges[b + 1], start_slot, 0)

    def drain(b):
        lax.fori_loop(edges[b], edges[b + 1], sent_slot, 0)

    used = [0]
    small_used = [0]

    def send(src, dst, device):
        slot = used[0]
        used[0] += 1
        copy = pltpu.make_async_remote_copy(
            src_ref=src, dst_ref=dst, send_sem=send_sem.at[slot], recv_sem=recv_sem.at[slot],
            device_id=device, device_id_type=MESH,
        )
        copy.start()
        return copy

    def send_small(peers, slots, mine):
        slots[mine] = small[...]
        copies = []
        for device, _ in peers:
            slot = small_used[0]
            small_used[0] += 1
            copy = pltpu.make_async_remote_copy(
                src_ref=small, dst_ref=slots.at[mine],
                send_sem=small_send.at[slot], recv_sem=small_recv.at[slot],
                device_id=device, device_id_type=MESH,
            )
            copy.start()
            copies.append(copy)
        return copies

    def add_small(copies, slots):
        for copy in copies:
            copy.wait()
        total = slots[0]
        for k in range(1, slots.shape[0]):
            total += slots[k]
        small[...] = total

    def columns(index, width):
        return pl.ds(pl.multiple_of(index * width, width), width)

    def lines(index, height):
        return pl.ds(pl.multiple_of(index * height, height), height)

    small[...] = s_ref[...]
    copies = [
        send(q_ref.at[lines(i, band_h), :], in_z.at[k], device) for k, (device, i) in enumerate(by_z)
    ]
    small_copies = send_small(by_z, small_z, z)
    own_slot = pltpu.make_async_copy(back_ref.at[me], arrived_ref.at[me], own_sem)
    own_slot.start()
    issue(0)
    issue(1)
    for copy in copies:
        copy.wait()
    total = q_ref[lines(z, band_h), :].astype(F32)
    for k in range(nz - 1):
        total += in_z[k].astype(F32)
    band[...] = total.astype(BF16)
    copies = [
        send(band.at[lines(i, piece_h), :], in_x.at[k], device) for k, (device, i) in enumerate(by_x)
    ]
    add_small(small_copies, small_z)
    small_copies = send_small(by_x, small_x, x)
    drain(0)
    issue(2)
    for copy in copies:
        copy.wait()
    total = band[lines(x, piece_h), :].astype(F32)
    for k in range(nx - 1):
        total += in_x[k].astype(F32)

    column = columns(core * ny + y, part_w)
    first = pl.multiple_of(z * band_h + x * piece_h, piece_h)
    out_ref[pl.ds(first, piece_h), column] = total.astype(BF16)

    def spread(peers, view):
        return [send(view, view, device) for device, _ in peers]

    copies = spread(by_x, out_ref.at[pl.ds(first, piece_h), column])
    add_small(small_copies, small_x)
    small_copies = send_small(by_y, small_y, y)
    drain(1)
    issue(3)
    for copy in copies:
        copy.wait()
    copies = spread(by_z, out_ref.at[lines(z, band_h), column])
    add_small(small_copies, small_y)
    small_copies = send_small(by_core, small_core, core)
    drain(2)
    issue(4)
    for copy in copies:
        copy.wait()
    own = out_ref.at[:, column]
    if ny == 4:
        turn = 1 - 2 * core
        ahead = at(x, lax.rem(y + turn + ny, ny), z, core)
        behind = at(x, lax.rem(y - turn + ny, ny), z, core)
        forth, back = send(own, own, ahead), send(own, own, behind)
        drain(3)
        issue(5)
        forth.wait()
        came = out_ref.at[:, columns(core * ny + lax.rem(y - turn + ny, ny), part_w)]
        copies = [back, send(came, came, ahead)]
    else:
        copies = spread(by_y, own)
        drain(3)
        issue(5)
    add_small(small_copies, small_core)
    t_ref[...] = small[...]
    drain(4)
    issue(6)
    for copy in copies:
        copy.wait()
    copies = spread(by_core, out_ref.at[:, columns(core, half_w)])
    drain(5)
    issue(7)
    drain(6)
    issue(8)
    for copy in copies:
        copy.wait()
    own_slot.wait()
    drain(7)
    drain(8)
    lax.fori_loop(0, count - 1, came_slot, 0)


def give_back(quarter, small, back, sizes):
    nx, ny, nz = sizes
    rows, part = quarter.shape
    count = back.shape[0]
    peers = 1 + (ny - 1) + (nz - 1) + (nx - 1)
    vmem = pl.BlockSpec(memory_space=pltpu.VMEM)
    anywhere = pl.BlockSpec(memory_space=pl.ANY)
    buffers = [
        (rows // nz, part), (nz - 1, rows // nz, part), (max(nx - 1, 1), rows // nz // nx, part),
    ]
    return pl.pallas_call(
        functools.partial(return_kernel, sizes, count),
        in_specs=[vmem, vmem, anywhere],
        out_specs=[vmem, vmem, anywhere],
        out_shape=[
            jax.ShapeDtypeStruct((rows, part * ny * 2), BF16),
            jax.ShapeDtypeStruct(small.shape, F32),
            jax.ShapeDtypeStruct(back.shape, BF16),
        ],
        scratch_shapes=[pltpu.VMEM(shape, BF16) for shape in buffers]
        + [pltpu.VMEM(small.shape, F32)]
        + [pltpu.VMEM((n,) + small.shape, F32) for n in (2, ny, nz, nx)]
        + [
            pltpu.SemaphoreType.DMA((2 * peers,)),
            pltpu.SemaphoreType.DMA((2 * peers,)),
            pltpu.SemaphoreType.DMA((peers,)),
            pltpu.SemaphoreType.DMA((peers,)),
            pltpu.SemaphoreType.DMA((2, count)),
            pltpu.SemaphoreType.DMA,
        ],
        compiler_params=params(collective_id=0, has_side_effects=True),
        name="give_back",
    )(quarter, small, back)


def scatter_core(normed, d, mixed, cot):
    pts = lax.axis_size("pts")
    core = lax.rem(lax.axis_index("pts"), 2)
    swap = [(source, source ^ 1) for source in range(pts)]
    theirs = lax.ppermute(weight_grad(1 - core, normed, d, mixed, cot), "pts", swap)
    return (
        weight_grad(core, normed, d, mixed, cot).astype(F32) + theirs.astype(F32)
    ).astype(BF16)


def scatter_rep(half):
    reps = lax.axis_size("rep")
    y = lax.axis_index("rep")

    def piece(step):
        return lax.dynamic_index_in_dim(half, lax.rem(y + step, reps), 0, keepdims=False)

    total = piece(0).astype(F32)
    for step in range(1, reps):
        total += shifted(piece(step), "rep", step).astype(F32)
    return total.astype(BF16)


def route_slots(rank_row, point_count, total, row_count, shard_count, send_size, offset):
    slot_total = rank_row.shape[0]
    index = jnp.arange(slot_total, dtype=jnp.int32)
    live_slot = index < point_count
    moved = rank_row % total
    target_shard = jnp.where(live_slot, moved // row_count, shard_count)
    matches = target_shard[:, None] == jnp.arange(shard_count, dtype=jnp.int32)[None, :]
    earlier = (index[:, None] > index[None, :]).astype(BF16)
    before = jnp.dot(earlier, matches.astype(BF16), preferred_element_type=F32)
    ordinal = jnp.sum(jnp.where(matches, before, 0.0), axis=1).astype(jnp.int32)
    target = jnp.where(live_slot, target_shard * send_size + ordinal, shard_count * send_size)
    return target, (moved % row_count - offset) % row_count


def on_device(
    sizes, points, counts, hilbert_rank, patch_shift, norm_gain, project_in, project_out, cotangent
):
    shard_count = lax.axis_size("pts")
    row_count = cotangent.shape[1]
    width = points.shape[2]
    slot_total = points.shape[1]
    slot_size = slot_total // shard_count
    total = row_count * shard_count
    offset = patch_shift[0]
    limit = row_count - offset
    own_row = jnp.arange(row_count, dtype=jnp.int32)[:, None] < limit

    cot_rows = cotangent[0]
    cot_next = shifted(cot_rows, "pts", -1)

    target, position = route_slots(
        hilbert_rank[0], counts[0, 0], total, row_count, shard_count, slot_size, offset
    )
    slot = jnp.arange(slot_total, dtype=jnp.int32)
    out_position = jnp.max(
        jnp.where(target[:, None] == slot[None, :], position[:, None], -1), axis=0
    )
    outgoing = place(target, points[0], slot_total)
    outgoing, cot_next = lax.optimization_barrier((outgoing, cot_next))
    lanes = -(-slot_size // 128) * 128
    sent_position = jnp.pad(
        out_position.reshape(shard_count, 1, slot_size),
        ((0, 0), (0, 0), (0, lanes - slot_size)),
        constant_values=-1,
    )
    incoming, in_position = deliver(
        outgoing.reshape(shard_count, slot_size, width), sent_position
    )
    incoming = incoming.reshape(slot_total, width)
    in_position = in_position[:, 0, :slot_size].reshape(slot_total)

    cot_window = lax.dynamic_slice_in_dim(
        jnp.concatenate([cot_rows, cot_next], axis=0), offset, row_count, 0
    )
    grad_mixed = jnp.dot(cot_window, project_out.T, preferred_element_type=F32).astype(BF16)

    rolled = place(in_position, incoming, row_count)
    rolled_next = shifted(rolled, "pts", -1)
    target_column = target.reshape(slot_total, 1)
    position_column = in_position.reshape(slot_total, 1)
    rolled_next, target_column, position_column, grad_mixed = lax.optimization_barrier(
        (rolled_next, target_column, position_column, grad_mixed)
    )
    window, normed, qkv = project(limit.reshape(1), rolled, rolled_next, norm_gain, project_in)
    mixed, d_qkv = attend(qkv, grad_mixed)
    grad_window, scale = input_grad(d_qkv, project_in, window, cot_window, norm_gain)
    grad_back = shifted(grad_window, "pts", 1)

    half = scatter_core(normed, d_qkv, mixed, cot_window)
    block_window = (
        window.astype(F32) + jnp.dot(mixed, project_out, preferred_element_type=F32)
    ).astype(BF16)
    grad_back, half, block_window = lax.optimization_barrier((grad_back, half, block_window))
    quarter = scatter_rep(half)
    block_back = shifted(block_window, "pts", 1)

    grad_rolled = jnp.where(own_row, grad_window, grad_back)
    returning = fetch(position_column, grad_rolled)
    small = jnp.zeros((8, 128), F32).at[: width // 128].set(scale.reshape(width // 128, 128))
    summed, small, arrived = give_back(
        quarter, small, returning.reshape(shard_count, slot_size, width), sizes
    )
    arrived = arrived.reshape(slot_total, width)

    block_rows = lax.dynamic_slice_in_dim(
        jnp.concatenate([block_back, block_window], axis=0), limit, row_count, 0
    )
    grad_points = fetch(target_column, arrived)
    factor = 1.0 / math.sqrt(total * lax.axis_size("rep"))
    return (
        block_rows[None],
        grad_points[None],
        summed[:, : 3 * width].astype(F32) * factor,
        summed[:, 3 * width :].astype(F32) * factor,
        small[: width // 128].reshape(width) * factor,
    )


def solution(mesh):
    spread = mesh.shape["pts"]
    sizes = {64: (4, 4, 8), 8: (2, 2, 2), 4: (1, 4, 2)}[spread]
    return jax.shard_map(
        functools.partial(on_device, sizes),
        mesh=mesh,
        in_specs=(
            P("rep", "pts", None),
            P("rep", "pts"),
            P("rep", "pts"),
            P("rep"),
            P(),
            P(),
            P(),
            P("rep", "pts", None),
        ),
        out_specs=(P("rep", "pts", None), P("rep", "pts", None), P(), P(), P()),
        check_vma=False,
    )
```

```python
import functools
import math

import jax
import jax.numpy as jnp
from jax import lax
from jax.experimental import pallas as pl
from jax.experimental.pallas import tpu as pltpu
from jax.sharding import PartitionSpec as P


HEAD_DIM = 64
EPSILON = 1e-05
MESH = pl.DeviceIdType.MESH
BF16 = jnp.bfloat16
F32 = jnp.float32
NT = (((1,), (1,)), ((), ()))
TN = (((0,), (0,)), ((), ()))


def params(**kw):
    return pltpu.CompilerParams(vmem_limit_bytes=56 << 20, **kw)


def shifted(value, axis, steps):
    count = lax.axis_size(axis)
    pairs = [(source, (source + steps) % count) for source in range(count)]
    return lax.ppermute(value, axis, pairs)


def place_kernel(dest_ref, src_ref, out_ref):
    block, depth = out_ref.shape[0], src_ref.shape[0]
    row = lax.broadcasted_iota(jnp.int32, (block, depth), 0) + pl.program_id(0) * block
    hot = jnp.where(row == dest_ref[...], 1.0, 0.0).astype(BF16)
    out_ref[...] = jnp.dot(hot, src_ref[...], preferred_element_type=F32).astype(BF16)


def place(dest, src, rows, block=512):
    depth, width = src.shape
    return pl.pallas_call(
        place_kernel,
        grid=(rows // block,),
        in_specs=[
            pl.BlockSpec((1, depth), lambda i: (0, 0)),
            pl.BlockSpec((depth, width), lambda i: (0, 0)),
        ],
        out_specs=pl.BlockSpec((block, width), lambda i: (i, 0)),
        out_shape=jax.ShapeDtypeStruct((rows, width), BF16),
        compiler_params=params(),
        name="place",
    )(dest.reshape(1, depth), src)


def fetch_kernel(index_ref, src_ref, out_ref):
    block, depth = out_ref.shape[0], src_ref.shape[0]
    column = lax.broadcasted_iota(jnp.int32, (block, depth), 1)
    hot = jnp.where(column == index_ref[...], 1.0, 0.0).astype(BF16)
    out_ref[...] = jnp.dot(hot, src_ref[...], preferred_element_type=F32).astype(BF16)


def fetch(index, src, block=512):
    depth, width = src.shape
    rows = index.shape[0]
    assert index.shape == (rows, 1)
    return pl.pallas_call(
        fetch_kernel,
        grid=(rows // block,),
        in_specs=[
            pl.BlockSpec((block, 1), lambda i: (i, 0)),
            pl.BlockSpec((depth, width), lambda i: (0, 0)),
        ],
        out_specs=pl.BlockSpec((block, width), lambda i: (i, 0)),
        out_shape=jax.ShapeDtypeStruct((rows, width), BF16),
        compiler_params=params(),
        name="fetch",
    )(index, src)


def deliver_kernel(count, out_ref, pos_ref, in_ref, in_pos_ref, sems, own_sems):
    me = lax.axis_index("pts")
    barrier = pltpu.get_barrier_semaphore()

    def greet(k, carry):
        pl.semaphore_signal(
            barrier, inc=1, device_id={"pts": lax.rem(me + k, count)}, device_id_type=MESH
        )
        return carry

    lax.fori_loop(1, count, greet, 0)
    pl.semaphore_wait(barrier, count - 1)
    own = [
        pltpu.make_async_copy(pos_ref.at[me], in_pos_ref.at[me], own_sems.at[0]),
        pltpu.make_async_copy(out_ref.at[me], in_ref.at[me], own_sems.at[1]),
    ]
    for copy in own:
        copy.start()

    def copies(j):
        near = j // 2 + 1
        k = near + lax.rem(j, 2) * (count - 2 * near)
        peer = lax.rem(me + k, count)
        return [
            pltpu.make_async_remote_copy(
                src_ref=src.at[peer], dst_ref=dst.at[me],
                send_sem=sems.at[2 * row, k], recv_sem=sems.at[2 * row + 1, k],
                device_id={"pts": peer}, device_id_type=MESH,
            )
            for row, (src, dst) in enumerate(((pos_ref, in_pos_ref), (out_ref, in_ref)))
        ]

    def start(j, carry):
        for copy in copies(j):
            copy.start()
        return carry

    def finish(j, carry):
        for copy in copies(j):
            copy.wait()
        return carry

    lax.fori_loop(0, count - 1, start, 0)
    lax.fori_loop(0, count - 1, finish, 0)
    for copy in own:
        copy.wait()


def deliver(outgoing, position):
    count = outgoing.shape[0]
    anywhere = pl.BlockSpec(memory_space=pl.ANY)
    return pl.pallas_call(
        functools.partial(deliver_kernel, count),
        in_specs=[anywhere, anywhere],
        out_specs=[anywhere, anywhere],
        out_shape=[
            jax.ShapeDtypeStruct(outgoing.shape, outgoing.dtype),
            jax.ShapeDtypeStruct(position.shape, position.dtype),
        ],
        scratch_shapes=[pltpu.SemaphoreType.DMA((4, count)), pltpu.SemaphoreType.DMA((2,))],
        compiler_params=params(collective_id=1, has_side_effects=True),
        name="deliver",
    )(outgoing, position)


def finish_kernel(index_ref, src_ref, grad_ref, out_ref, in_ref, outer_ref, *, factor):
    fetch_kernel(index_ref, src_ref, out_ref)
    inner = in_ref.shape[1]
    in_ref[...] = grad_ref[:, :inner].astype(F32) * factor
    outer_ref[...] = grad_ref[:, inner:].astype(F32) * factor


def finish(index, src, grads, factor, steps=4):
    depth, width = src.shape
    rows, tall = index.shape[0], grads.shape[0]
    block, part = rows // steps, tall // steps
    inner = grads.shape[1] - width
    return pl.pallas_call(
        functools.partial(finish_kernel, factor=factor),
        grid=(steps,),
        in_specs=[
            pl.BlockSpec((block, 1), lambda i: (i, 0)),
            pl.BlockSpec((depth, width), lambda i: (0, 0)),
            pl.BlockSpec((part, inner + width), lambda i: (i, 0)),
        ],
        out_specs=[
            pl.BlockSpec((block, width), lambda i: (i, 0)),
            pl.BlockSpec((part, inner), lambda i: (i, 0)),
            pl.BlockSpec((part, width), lambda i: (i, 0)),
        ],
        out_shape=[
            jax.ShapeDtypeStruct((rows, width), BF16),
            jax.ShapeDtypeStruct((tall, inner), F32),
            jax.ShapeDtypeStruct((tall, width), F32),
        ],
        compiler_params=params(),
        name="finish",
    )(index, src, grads)


def unit_of(values):
    centre = jnp.mean(values, axis=-1, keepdims=True)
    deviation = values - centre
    inverse = lax.rsqrt(jnp.mean(deviation * deviation, axis=-1, keepdims=True) + EPSILON)
    return deviation * inverse, inverse


def project_kernel(limit_ref, own_ref, next_ref, gain_ref, weight_ref, win_ref, normed_ref, qkv_ref):
    block = own_ref.shape[0]
    row = lax.broadcasted_iota(jnp.int32, own_ref.shape, 0) + pl.program_id(0) * block
    values = jnp.where(
        row < limit_ref[0], own_ref[...].astype(F32), next_ref[...].astype(F32)
    )
    unit, _ = unit_of(values)
    normed = (unit * gain_ref[...]).astype(BF16)
    win_ref[...] = values.astype(BF16)
    normed_ref[...] = normed
    qkv_ref[...] = jnp.dot(normed, weight_ref[...], preferred_element_type=F32).astype(BF16)


def project(limit, own, following, gain, weight, block=512):
    rows, width = own.shape
    wide = weight.shape[1]
    tile = pl.BlockSpec((block, width), lambda i: (i, 0))
    return pl.pallas_call(
        project_kernel,
        grid=(rows // block,),
        in_specs=[
            pl.BlockSpec(memory_space=pltpu.SMEM),
            tile,
            tile,
            pl.BlockSpec((1, width), lambda i: (0, 0)),
            pl.BlockSpec((width, wide), lambda i: (0, 0)),
        ],
        out_specs=[tile, tile, pl.BlockSpec((block, wide), lambda i: (i, 0))],
        out_shape=[
            jax.ShapeDtypeStruct((rows, width), BF16),
            jax.ShapeDtypeStruct((rows, width), BF16),
            jax.ShapeDtypeStruct((rows, wide), BF16),
        ],
        compiler_params=params(),
        name="project",
    )(limit, own, following, gain.reshape(1, width), weight)


def attend_kernel(q_ref, k_ref, v_ref, g_ref, mixed_ref, d_ref, dk_ref, dv_ref, *, chunk):
    rows = q_ref.shape[0]
    keys, values = k_ref[...], v_ref[...]
    lane = lax.broadcasted_iota(jnp.int32, (1, 128), 1)
    line = lax.broadcasted_iota(jnp.int32, (128, 1), 0)
    lanes = [jnp.where(lane < HEAD_DIM, 1.0, 0.0), jnp.where(lane < HEAD_DIM, 0.0, 1.0)]
    lines = [jnp.where(line < HEAD_DIM, 1.0, 0.0), jnp.where(line < HEAD_DIM, 0.0, 1.0)]
    keys_t = keys.astype(F32).T
    values_t = values.astype(F32).T
    keys_t = [(keys_t * m).astype(BF16) for m in lines]
    values_t = [(values_t * m).astype(BF16) for m in lines]
    steps = rows // chunk
    for at in range(steps):
        window = slice(at * chunk, (at + 1) * chunk)
        q_all = q_ref[window, :].astype(F32) * HEAD_DIM ** (-0.5)
        g_all = g_ref[window, :].astype(F32)
        q = jnp.concatenate([(q_all * m).astype(BF16) for m in lanes], axis=0)
        g = jnp.concatenate([(g_all * m).astype(BF16) for m in lanes], axis=0)
        logits = lax.dot_general(keys, q, NT, preferred_element_type=F32)
        power = jnp.exp(logits - jnp.max(logits, axis=0, keepdims=True))
        share = power * (1.0 / jnp.sum(power, axis=0, keepdims=True))
        share_b = share.astype(BF16)
        dshare = lax.dot_general(values, g, NT, preferred_element_type=F32)
        dot = jnp.sum(dshare * share, axis=0, keepdims=True)
        dlogits = (share * (dshare - dot)).astype(BF16)
        mixed_t = jnp.zeros((128, chunk), F32)
        dq_t = jnp.zeros((128, chunk), F32)
        for head in range(2):
            part = slice(head * chunk, (head + 1) * chunk)
            mixed_t += jnp.dot(values_t[head], share_b[:, part], preferred_element_type=F32)
            dq_t += jnp.dot(keys_t[head], dlogits[:, part], preferred_element_type=F32)
        dv = jnp.dot(share_b, g, preferred_element_type=F32)
        dk = jnp.dot(dlogits, q, preferred_element_type=F32)
        if at > 0:
            dv += dv_ref[...]
            dk += dk_ref[...]
        if at < steps - 1:
            dv_ref[...] = dv
            dk_ref[...] = dk
        else:
            d_ref[1] = dk.astype(BF16)
            d_ref[2] = dv.astype(BF16)
        mixed_ref[window, :] = mixed_t.T.astype(BF16)
        d_ref[0, window, :] = (dq_t * HEAD_DIM ** (-0.5)).T.astype(BF16)


def attend(qkv, grads, chunk=512):
    rows, width = grads.shape
    pairs = width // 128
    return pl.pallas_call(
        functools.partial(attend_kernel, chunk=chunk),
        grid=(pairs,),
        in_specs=[
            pl.BlockSpec((rows, 128), lambda j: (0, j)),
            pl.BlockSpec((rows, 128), lambda j: (0, pairs + j)),
            pl.BlockSpec((rows, 128), lambda j: (0, 2 * pairs + j)),
            pl.BlockSpec((rows, 128), lambda j: (0, j)),
        ],
        out_specs=[
            pl.BlockSpec((rows, 128), lambda j: (0, j)),
            pl.BlockSpec((3, rows, 128), lambda j: (0, 0, j)),
        ],
        out_shape=[
            jax.ShapeDtypeStruct((rows, width), BF16),
            jax.ShapeDtypeStruct((3, rows, width), BF16),
        ],
        scratch_shapes=[pltpu.VMEM((rows, 128), F32), pltpu.VMEM((rows, 128), F32)],
        compiler_params=params(),
        name="attend",
    )(qkv, qkv, qkv, grads)


def input_grad_kernel(d_ref, weight_ref, win_ref, cot_ref, gain_ref, out_ref, scale_ref):
    width = win_ref.shape[1]
    grad = jnp.zeros(win_ref.shape, F32)
    for part in range(3):
        grad += lax.dot_general(
            d_ref[part],
            weight_ref[:, part * width : (part + 1) * width],
            NT,
            preferred_element_type=F32,
        )
    unit, inverse = unit_of(win_ref[...].astype(F32))
    product = grad * unit

    @pl.when(pl.program_id(0) == 0)
    def _():
        scale_ref[...] = jnp.zeros_like(scale_ref)

    scale_ref[...] += jnp.sum(product, axis=0, keepdims=True)
    weighted = grad * gain_ref[...]
    branch = inverse * (
        weighted
        - jnp.mean(weighted, axis=-1, keepdims=True)
        - unit * jnp.mean(product * gain_ref[...], axis=-1, keepdims=True)
    )
    out_ref[...] = (cot_ref[...].astype(F32) + branch).astype(BF16)


def input_grad(d, weight, win, cot, gain, block=512):
    rows, width = win.shape
    tile = pl.BlockSpec((block, width), lambda i: (i, 0))
    return pl.pallas_call(
        input_grad_kernel,
        grid=(rows // block,),
        in_specs=[
            pl.BlockSpec((3, block, width), lambda i: (0, i, 0)),
            pl.BlockSpec(weight.shape, lambda i: (0, 0)),
            tile,
            tile,
            pl.BlockSpec((1, width), lambda i: (0, 0)),
        ],
        out_specs=[tile, pl.BlockSpec((1, width), lambda i: (0, 0))],
        out_shape=[
            jax.ShapeDtypeStruct((rows, width), BF16),
            jax.ShapeDtypeStruct((1, width), F32),
        ],
        compiler_params=params(),
        name="input_grad",
    )(d, weight, win, cot, gain.reshape(1, width))


def weight_grad_kernel(half_ref, normed_ref, d_ref, mixed_ref, cot_ref, out_ref):
    part = half_ref[0] * 2 + pl.program_id(0)
    middle = out_ref.shape[2]

    def emit(left, right):
        grad = lax.dot_general(left, right, TN, preferred_element_type=F32).astype(BF16)
        out_ref[0] = grad[:, :middle]
        out_ref[1] = grad[:, middle:]

    @pl.when(part < 3)
    def _():
        emit(normed_ref[...], d_ref[0])

    @pl.when(part == 3)
    def _():
        emit(mixed_ref[...], cot_ref[...])


def weight_grad(half, normed, d, mixed, cot):
    rows, width = normed.shape
    whole = pl.BlockSpec((rows, width), lambda j, half: (0, 0))
    return pl.pallas_call(
        weight_grad_kernel,
        grid_spec=pltpu.PrefetchScalarGridSpec(
            num_scalar_prefetch=1,
            grid=(2,),
            in_specs=[
                whole,
                pl.BlockSpec(
                    (1, rows, width), lambda j, half: (jnp.minimum(half[0] * 2 + j, 2), 0, 0)
                ),
                whole,
                whole,
            ],
            out_specs=pl.BlockSpec((2, width, width // 2), lambda j, half: (j, 0, 0)),
        ),
        out_shape=jax.ShapeDtypeStruct((4, width, width // 2), BF16),
        compiler_params=params(),
        name="weight_grad",
    )(half.reshape(1), normed, d, mixed, cot)


def return_kernel(
    sizes, count, q_ref, s_ref, back_ref, out_ref, t_ref, arrived_ref,
    band, in_x, in_z, small, small_core, small_y, small_z, small_x,
    send_sem, recv_sem, small_send, small_recv, slot_sems, own_sem,
):
    nx, ny, nz = sizes
    rows, part_w = q_ref.shape
    half_w = part_w * ny
    band_h, piece_h = rows // nx, rows // nx // nz
    me = lax.axis_index("pts")
    y = lax.axis_index("rep")
    core = lax.rem(me, 2)
    z = lax.rem(me // 2, nz)
    x = me // (2 * nz)

    def at(x_, y_, z_, core_):
        return {"pts": (x_ * nz + z_) * 2 + core_, "rep": y_}

    by_core = [(at(x, y, z, 1 - core), 1 - core)]
    by_y = [(at(x, lax.rem(y + k, ny), z, core), lax.rem(y + k, ny)) for k in range(1, ny)]
    by_z = [(at(x, y, lax.rem(z + k, nz), core), lax.rem(z + k, nz)) for k in range(1, nz)]
    by_x = [(at(lax.rem(x + k, nx), y, z, core), lax.rem(x + k, nx)) for k in range(1, nx)]
    barrier = pltpu.get_barrier_semaphore()

    def greet(k, carry):
        pl.semaphore_signal(
            barrier, inc=1, device_id={"pts": lax.rem(me + k, count)}, device_id_type=MESH
        )
        return carry

    lax.fori_loop(1, count, greet, 0)
    for device, _ in by_y:
        pl.semaphore_signal(barrier, inc=1, device_id=device, device_id_type=MESH)
    pl.semaphore_wait(barrier, count - 1 + len(by_y))

    def slot_copy(j):
        near = j // 2 + 1
        k = near + lax.rem(j, 2) * (count - 2 * near)
        peer = lax.rem(me + k, count)
        return pltpu.make_async_remote_copy(
            src_ref=back_ref.at[peer], dst_ref=arrived_ref.at[me],
            send_sem=slot_sems.at[0, k], recv_sem=slot_sems.at[1, k],
            device_id={"pts": peer}, device_id_type=MESH,
        )

    batches = 9
    edges = [(count - 1) * b // batches for b in range(batches + 1)]

    def start_slot(j, carry):
        slot_copy(j).start()
        return carry

    def sent_slot(j, carry):
        slot_copy(j).wait_send()
        return carry

    def came_slot(j, carry):
        slot_copy(j).wait_recv()
        return carry

    def issue(b):
        lax.fori_loop(edges[b], edges[b + 1], start_slot, 0)

    def drain(b):
        lax.fori_loop(edges[b], edges[b + 1], sent_slot, 0)

    used = [0]
    small_used = [0]

    def send(src, dst, device):
        slot = used[0]
        used[0] += 1
        copy = pltpu.make_async_remote_copy(
            src_ref=src, dst_ref=dst, send_sem=send_sem.at[slot], recv_sem=recv_sem.at[slot],
            device_id=device, device_id_type=MESH,
        )
        copy.start()
        return copy

    def send_small(peers, slots, mine):
        slots[mine] = small[...]
        copies = []
        for device, _ in peers:
            slot = small_used[0]
            small_used[0] += 1
            copy = pltpu.make_async_remote_copy(
                src_ref=small, dst_ref=slots.at[mine],
                send_sem=small_send.at[slot], recv_sem=small_recv.at[slot],
                device_id=device, device_id_type=MESH,
            )
            copy.start()
            copies.append(copy)
        return copies

    def add_small(copies, slots):
        for copy in copies:
            copy.wait()
        total = slots[0]
        for k in range(1, slots.shape[0]):
            total += slots[k]
        small[...] = total

    def columns(index, width):
        return pl.ds(pl.multiple_of(index * width, width), width)

    def lines(index, height):
        return pl.ds(pl.multiple_of(index * height, height), height)

    small[...] = s_ref[...]
    copies = [
        send(q_ref.at[lines(i, band_h), :], in_x.at[k], device) for k, (device, i) in enumerate(by_x)
    ]
    small_copies = send_small(by_x, small_x, x)
    own_slot = pltpu.make_async_copy(back_ref.at[me], arrived_ref.at[me], own_sem)
    own_slot.start()
    issue(0)
    issue(1)
    for copy in copies:
        copy.wait()
    total = q_ref[lines(x, band_h), :].astype(F32)
    for k in range(nx - 1):
        total += in_x[k].astype(F32)
    band[...] = total.astype(BF16)
    copies = [
        send(band.at[lines(i, piece_h), :], in_z.at[k], device) for k, (device, i) in enumerate(by_z)
    ]
    add_small(small_copies, small_x)
    small_copies = send_small(by_z, small_z, z)
    drain(0)
    issue(2)
    for copy in copies:
        copy.wait()
    total = band[lines(z, piece_h), :].astype(F32)
    for k in range(nz - 1):
        total += in_z[k].astype(F32)

    column = columns(core * ny + y, part_w)
    first = pl.multiple_of(x * band_h + z * piece_h, piece_h)
    out_ref[pl.ds(first, piece_h), column] = total.astype(BF16)

    def spread(peers, view):
        return [send(view, view, device) for device, _ in peers]

    copies = spread(by_z, out_ref.at[pl.ds(first, piece_h), column])
    add_small(small_copies, small_z)
    small_copies = send_small(by_y, small_y, y)
    drain(1)
    issue(3)
    for copy in copies:
        copy.wait()
    copies = spread(by_x, out_ref.at[lines(x, band_h), column])
    add_small(small_copies, small_y)
    small_copies = send_small(by_core, small_core, core)
    drain(2)
    issue(4)
    for copy in copies:
        copy.wait()
    own = out_ref.at[:, column]
    if ny == 4:
        turn = 1 - 2 * core
        ahead = at(x, lax.rem(y + turn + ny, ny), z, core)
        behind = at(x, lax.rem(y - turn + ny, ny), z, core)

        def block(step):
            return out_ref.at[:, columns(core * ny + lax.rem(y + step * turn + ny, ny), part_w)]

        forth, back = send(own, own, ahead), send(own, own, behind)
        last = spread(by_core, own)
        drain(3)
        issue(5)
        forth.wait()
        passed = send(block(-1), block(-1), ahead)
        last += spread(by_core, block(-1))
        add_small(small_copies, small_core)
        t_ref[...] = small[...]
        drain(4)
        issue(6)
        back.wait()
        last += spread(by_core, block(1))
        passed.wait()
        last += spread(by_core, block(2))
    else:
        copies = spread(by_y, own)
        add_small(small_copies, small_core)
        t_ref[...] = small[...]
        drain(3)
        issue(5)
        drain(4)
        issue(6)
        for copy in copies:
            copy.wait()
        last = spread(by_core, out_ref.at[:, columns(core, half_w)])
    drain(5)
    issue(7)
    drain(6)
    issue(8)
    for copy in last:
        copy.wait()
    own_slot.wait()
    drain(7)
    drain(8)
    lax.fori_loop(0, count - 1, came_slot, 0)


def give_back(quarter, small, back, sizes):
    nx, ny, nz = sizes
    rows, part = quarter.shape
    count = back.shape[0]
    peers = 1 + (ny - 1) + (nz - 1) + (nx - 1)
    vmem = pl.BlockSpec(memory_space=pltpu.VMEM)
    anywhere = pl.BlockSpec(memory_space=pl.ANY)
    buffers = [
        (rows // nx, part), (max(nx - 1, 1), rows // nx, part), (nz - 1, rows // nx // nz, part),
    ]
    return pl.pallas_call(
        functools.partial(return_kernel, sizes, count),
        in_specs=[vmem, vmem, anywhere],
        out_specs=[vmem, vmem, anywhere],
        out_shape=[
            jax.ShapeDtypeStruct((rows, part * ny * 2), BF16),
            jax.ShapeDtypeStruct(small.shape, F32),
            jax.ShapeDtypeStruct(back.shape, BF16),
        ],
        scratch_shapes=[pltpu.VMEM(shape, BF16) for shape in buffers]
        + [pltpu.VMEM(small.shape, F32)]
        + [pltpu.VMEM((n,) + small.shape, F32) for n in (2, ny, nz, nx)]
        + [
            pltpu.SemaphoreType.DMA((2 * peers + ny,)),
            pltpu.SemaphoreType.DMA((2 * peers + ny,)),
            pltpu.SemaphoreType.DMA((peers,)),
            pltpu.SemaphoreType.DMA((peers,)),
            pltpu.SemaphoreType.DMA((2, count)),
            pltpu.SemaphoreType.DMA,
        ],
        compiler_params=params(collective_id=0, has_side_effects=True),
        name="give_back",
    )(quarter, small, back)


def scatter_core(normed, d, mixed, cot):
    pts = lax.axis_size("pts")
    core = lax.rem(lax.axis_index("pts"), 2)
    swap = [(source, source ^ 1) for source in range(pts)]
    sent = weight_grad(1 - core, normed, d, mixed, cot)
    theirs = lax.ppermute(sent, "pts", swap)
    return (
        weight_grad(core, normed, d, mixed, cot).astype(F32) + theirs.astype(F32)
    ).astype(BF16)


def scatter_rep(half):
    reps = lax.axis_size("rep")
    y = lax.axis_index("rep")

    def piece(step):
        return lax.dynamic_index_in_dim(half, lax.rem(y + step, reps), 0, keepdims=False)

    total = piece(0).astype(F32)
    for step in range(1, reps):
        total += shifted(piece(step), "rep", step).astype(F32)
    return total.astype(BF16)


def route_slots(rank_row, point_count, total, row_count, shard_count, send_size, offset):
    slot_total = rank_row.shape[0]
    index = jnp.arange(slot_total, dtype=jnp.int32)
    live_slot = index < point_count
    moved = rank_row % total
    target_shard = jnp.where(live_slot, moved // row_count, shard_count)
    matches = target_shard[:, None] == jnp.arange(shard_count, dtype=jnp.int32)[None, :]
    earlier = (index[:, None] > index[None, :]).astype(BF16)
    before = jnp.dot(earlier, matches.astype(BF16), preferred_element_type=F32)
    ordinal = jnp.sum(jnp.where(matches, before, 0.0), axis=1).astype(jnp.int32)
    target = jnp.where(live_slot, target_shard * send_size + ordinal, shard_count * send_size)
    return target, (moved % row_count - offset) % row_count


def on_device(
    sizes, points, counts, hilbert_rank, patch_shift, norm_gain, project_in, project_out, cotangent
):
    shard_count = lax.axis_size("pts")
    row_count = cotangent.shape[1]
    width = points.shape[2]
    slot_total = points.shape[1]
    slot_size = slot_total // shard_count
    total = row_count * shard_count
    offset = patch_shift[0]
    limit = row_count - offset
    own_row = jnp.arange(row_count, dtype=jnp.int32)[:, None] < limit

    cot_rows = cotangent[0]
    cot_next = shifted(cot_rows, "pts", -1)

    target, position = route_slots(
        hilbert_rank[0], counts[0, 0], total, row_count, shard_count, slot_size, offset
    )
    slot = jnp.arange(slot_total, dtype=jnp.int32)
    out_position = jnp.max(
        jnp.where(target[:, None] == slot[None, :], position[:, None], -1), axis=0
    )
    outgoing = place(target, points[0], slot_total)
    outgoing, cot_next = lax.optimization_barrier((outgoing, cot_next))
    lanes = -(-slot_size // 128) * 128
    sent_position = jnp.pad(
        out_position.reshape(shard_count, 1, slot_size),
        ((0, 0), (0, 0), (0, lanes - slot_size)),
        constant_values=-1,
    )
    incoming, in_position = deliver(
        outgoing.reshape(shard_count, slot_size, width), sent_position
    )
    incoming = incoming.reshape(slot_total, width)
    in_position = in_position[:, 0, :slot_size].reshape(slot_total)

    cot_window = lax.dynamic_slice_in_dim(
        jnp.concatenate([cot_rows, cot_next], axis=0), offset, row_count, 0
    )
    grad_mixed = jnp.dot(cot_window, project_out.T, preferred_element_type=F32).astype(BF16)

    rolled = place(in_position, incoming, row_count)
    rolled_next = shifted(rolled, "pts", -1)
    target_column = target.reshape(slot_total, 1)
    position_column = in_position.reshape(slot_total, 1)
    rolled_next, target_column, position_column, grad_mixed = lax.optimization_barrier(
        (rolled_next, target_column, position_column, grad_mixed)
    )
    window, normed, qkv = project(limit.reshape(1), rolled, rolled_next, norm_gain, project_in)
    mixed, d_qkv = attend(qkv, grad_mixed)
    grad_window, scale = input_grad(d_qkv, project_in, window, cot_window, norm_gain)
    grad_back = shifted(grad_window, "pts", 1)

    half = scatter_core(normed, d_qkv, mixed, cot_window)
    block_window = (
        window.astype(F32) + jnp.dot(mixed, project_out, preferred_element_type=F32)
    ).astype(BF16)
    grad_back, half, block_window = lax.optimization_barrier((grad_back, half, block_window))
    quarter = scatter_rep(half)
    block_back = shifted(block_window, "pts", 1)

    grad_rolled = jnp.where(own_row, grad_window, grad_back)
    returning = fetch(position_column, grad_rolled)
    small = jnp.zeros((8, 128), F32).at[: width // 128].set(scale.reshape(width // 128, 128))
    summed, small, arrived = give_back(
        quarter, small, returning.reshape(shard_count, slot_size, width), sizes
    )
    arrived = arrived.reshape(slot_total, width)

    block_rows = lax.dynamic_slice_in_dim(
        jnp.concatenate([block_back, block_window], axis=0), limit, row_count, 0
    )
    factor = 1.0 / math.sqrt(total * lax.axis_size("rep"))
    grad_points, grad_in, grad_out = finish(target_column, arrived, summed, factor)
    return (
        block_rows[None],
        grad_points[None],
        grad_in,
        grad_out,
        small[: width // 128].reshape(width) * factor,
    )


def solution(mesh):
    spread = mesh.shape["pts"]
    sizes = {64: (4, 4, 8), 8: (2, 2, 2), 4: (1, 4, 2)}[spread]
    return jax.shard_map(
        functools.partial(on_device, sizes),
        mesh=mesh,
        in_specs=(
            P("rep", "pts", None),
            P("rep", "pts"),
            P("rep", "pts"),
            P("rep"),
            P(),
            P(),
            P(),
            P("rep", "pts", None),
        ),
        out_specs=(P("rep", "pts", None), P("rep", "pts", None), P(), P(), P()),
        check_vma=False,
    )
```

```python
import functools
import math

import jax
import jax.numpy as jnp
from jax import lax
from jax.experimental import pallas as pl
from jax.experimental.pallas import tpu as pltpu
from jax.sharding import PartitionSpec as P


HEAD_DIM = 64
EPSILON = 1e-05
MESH = pl.DeviceIdType.MESH
BATCHES = 9
LEAD = 4
BF16 = jnp.bfloat16
F32 = jnp.float32
NT = (((1,), (1,)), ((), ()))
TN = (((0,), (0,)), ((), ()))


def params(**kw):
    return pltpu.CompilerParams(vmem_limit_bytes=56 << 20, **kw)


def shifted(value, axis, steps):
    count = lax.axis_size(axis)
    pairs = [(source, (source + steps) % count) for source in range(count)]
    return lax.ppermute(value, axis, pairs)


def place_kernel(dest_ref, src_ref, out_ref):
    block, depth = out_ref.shape[0], src_ref.shape[0]
    row = lax.broadcasted_iota(jnp.int32, (block, depth), 0) + pl.program_id(0) * block
    hot = jnp.where(row == dest_ref[...], 1.0, 0.0).astype(BF16)
    out_ref[...] = jnp.dot(hot, src_ref[...], preferred_element_type=F32).astype(BF16)


def place(dest, src, rows, block=512):
    depth, width = src.shape
    return pl.pallas_call(
        place_kernel,
        grid=(rows // block,),
        in_specs=[
            pl.BlockSpec((1, depth), lambda i: (0, 0)),
            pl.BlockSpec((depth, width), lambda i: (0, 0)),
        ],
        out_specs=pl.BlockSpec((block, width), lambda i: (i, 0)),
        out_shape=jax.ShapeDtypeStruct((rows, width), BF16),
        compiler_params=params(),
        name="place",
    )(dest.reshape(1, depth), src)


def fetch_kernel(index_ref, src_ref, out_ref):
    block, depth = out_ref.shape[0], src_ref.shape[0]
    column = lax.broadcasted_iota(jnp.int32, (block, depth), 1)
    hot = jnp.where(column == index_ref[...], 1.0, 0.0).astype(BF16)
    out_ref[...] = jnp.dot(hot, src_ref[...], preferred_element_type=F32).astype(BF16)


def fetch(index, src, block=512):
    depth, width = src.shape
    rows = index.shape[0]
    assert index.shape == (rows, 1)
    return pl.pallas_call(
        fetch_kernel,
        grid=(rows // block,),
        in_specs=[
            pl.BlockSpec((block, 1), lambda i: (i, 0)),
            pl.BlockSpec((depth, width), lambda i: (0, 0)),
        ],
        out_specs=pl.BlockSpec((block, width), lambda i: (i, 0)),
        out_shape=jax.ShapeDtypeStruct((rows, width), BF16),
        compiler_params=params(),
        name="fetch",
    )(index, src)


def deliver_kernel(count, out_ref, pos_ref, in_ref, in_pos_ref, sems, own_sems):
    me = lax.axis_index("pts")
    barrier = pltpu.get_barrier_semaphore()

    def greet(k, carry):
        pl.semaphore_signal(
            barrier, inc=1, device_id={"pts": lax.rem(me + k, count)}, device_id_type=MESH
        )
        return carry

    lax.fori_loop(1, count, greet, 0)
    pl.semaphore_wait(barrier, count - 1)
    own = [
        pltpu.make_async_copy(pos_ref.at[me], in_pos_ref.at[me], own_sems.at[0]),
        pltpu.make_async_copy(out_ref.at[me], in_ref.at[me], own_sems.at[1]),
    ]
    for copy in own:
        copy.start()

    def copies(j):
        near = j // 2 + 1
        k = near + lax.rem(j, 2) * (count - 2 * near)
        peer = lax.rem(me + k, count)
        return [
            pltpu.make_async_remote_copy(
                src_ref=src.at[peer], dst_ref=dst.at[me],
                send_sem=sems.at[2 * row, k], recv_sem=sems.at[2 * row + 1, k],
                device_id={"pts": peer}, device_id_type=MESH,
            )
            for row, (src, dst) in enumerate(((pos_ref, in_pos_ref), (out_ref, in_ref)))
        ]

    def start(j, carry):
        for copy in copies(j):
            copy.start()
        return carry

    def finish(j, carry):
        for copy in copies(j):
            copy.wait()
        return carry

    lax.fori_loop(0, count - 1, start, 0)
    lax.fori_loop(0, count - 1, finish, 0)
    for copy in own:
        copy.wait()


def deliver(outgoing, position):
    count = outgoing.shape[0]
    anywhere = pl.BlockSpec(memory_space=pl.ANY)
    return pl.pallas_call(
        functools.partial(deliver_kernel, count),
        in_specs=[anywhere, anywhere],
        out_specs=[anywhere, anywhere],
        out_shape=[
            jax.ShapeDtypeStruct(outgoing.shape, outgoing.dtype),
            jax.ShapeDtypeStruct(position.shape, position.dtype),
        ],
        scratch_shapes=[pltpu.SemaphoreType.DMA((4, count)), pltpu.SemaphoreType.DMA((2,))],
        compiler_params=params(collective_id=1, has_side_effects=True),
        name="deliver",
    )(outgoing, position)


def finish_kernel(
    offset_ref, index_ref, src_ref, grad_ref, window_ref, back_ref,
    out_ref, in_ref, outer_ref, block_ref, *, factor,
):
    fetch_kernel(index_ref, src_ref, out_ref)
    rows = window_ref.shape[0]
    row = lax.broadcasted_iota(jnp.int32, window_ref.shape, 0)
    rolled = jnp.where(
        row < rows - offset_ref[0], window_ref[...].astype(F32), back_ref[...].astype(F32)
    )
    block_ref[...] = pltpu.roll(rolled, offset_ref[0], 0).astype(BF16)
    inner = in_ref.shape[1]
    in_ref[...] = grad_ref[:, :inner].astype(F32) * factor
    outer_ref[...] = grad_ref[:, inner:].astype(F32) * factor


def finish(offset, index, src, grads, window, back, factor, steps=4):
    depth, width = src.shape
    rows, tall = index.shape[0], grads.shape[0]
    block, part, lanes = rows // steps, tall // steps, width // steps
    inner = grads.shape[1] - width
    strip = pl.BlockSpec((window.shape[0], lanes), lambda i: (0, i))
    return pl.pallas_call(
        functools.partial(finish_kernel, factor=factor),
        grid=(steps,),
        in_specs=[
            pl.BlockSpec(memory_space=pltpu.SMEM),
            pl.BlockSpec((block, 1), lambda i: (i, 0)),
            pl.BlockSpec((depth, width), lambda i: (0, 0)),
            pl.BlockSpec((part, inner + width), lambda i: (i, 0)),
            strip,
            strip,
        ],
        out_specs=[
            pl.BlockSpec((block, width), lambda i: (i, 0)),
            pl.BlockSpec((part, inner), lambda i: (i, 0)),
            pl.BlockSpec((part, width), lambda i: (i, 0)),
            strip,
        ],
        out_shape=[
            jax.ShapeDtypeStruct((rows, width), BF16),
            jax.ShapeDtypeStruct((tall, inner), F32),
            jax.ShapeDtypeStruct((tall, width), F32),
            jax.ShapeDtypeStruct(window.shape, BF16),
        ],
        compiler_params=params(),
        name="finish",
    )(offset, index, src, grads, window, back)


def unit_of(values):
    centre = jnp.mean(values, axis=-1, keepdims=True)
    deviation = values - centre
    inverse = lax.rsqrt(jnp.mean(deviation * deviation, axis=-1, keepdims=True) + EPSILON)
    return deviation * inverse, inverse


def project_kernel(limit_ref, own_ref, next_ref, gain_ref, weight_ref, win_ref, normed_ref, qkv_ref):
    block = own_ref.shape[0]
    row = lax.broadcasted_iota(jnp.int32, own_ref.shape, 0) + pl.program_id(0) * block
    values = jnp.where(
        row < limit_ref[0], own_ref[...].astype(F32), next_ref[...].astype(F32)
    )
    unit, _ = unit_of(values)
    normed = (unit * gain_ref[...]).astype(BF16)
    win_ref[...] = values.astype(BF16)
    normed_ref[...] = normed
    qkv_ref[...] = jnp.dot(normed, weight_ref[...], preferred_element_type=F32).astype(BF16)


def project(limit, own, following, gain, weight, block=512):
    rows, width = own.shape
    wide = weight.shape[1]
    tile = pl.BlockSpec((block, width), lambda i: (i, 0))
    return pl.pallas_call(
        project_kernel,
        grid=(rows // block,),
        in_specs=[
            pl.BlockSpec(memory_space=pltpu.SMEM),
            tile,
            tile,
            pl.BlockSpec((1, width), lambda i: (0, 0)),
            pl.BlockSpec((width, wide), lambda i: (0, 0)),
        ],
        out_specs=[tile, tile, pl.BlockSpec((block, wide), lambda i: (i, 0))],
        out_shape=[
            jax.ShapeDtypeStruct((rows, width), BF16),
            jax.ShapeDtypeStruct((rows, width), BF16),
            jax.ShapeDtypeStruct((rows, wide), BF16),
        ],
        compiler_params=params(),
        name="project",
    )(limit, own, following, gain.reshape(1, width), weight)


def attend_kernel(q_ref, k_ref, v_ref, g_ref, mixed_ref, d_ref, dk_ref, dv_ref, *, chunk):
    rows = q_ref.shape[0]
    keys, values = k_ref[...], v_ref[...]
    lane = lax.broadcasted_iota(jnp.int32, (1, 128), 1)
    line = lax.broadcasted_iota(jnp.int32, (128, 1), 0)
    lanes = [jnp.where(lane < HEAD_DIM, 1.0, 0.0), jnp.where(lane < HEAD_DIM, 0.0, 1.0)]
    lines = [jnp.where(line < HEAD_DIM, 1.0, 0.0), jnp.where(line < HEAD_DIM, 0.0, 1.0)]
    keys_t = keys.astype(F32).T
    values_t = values.astype(F32).T
    keys_t = [(keys_t * m).astype(BF16) for m in lines]
    values_t = [(values_t * m).astype(BF16) for m in lines]
    steps = rows // chunk
    for at in range(steps):
        window = slice(at * chunk, (at + 1) * chunk)
        q_all = q_ref[window, :].astype(F32) * HEAD_DIM ** (-0.5)
        g_all = g_ref[window, :].astype(F32)
        q = jnp.concatenate([(q_all * m).astype(BF16) for m in lanes], axis=0)
        g = jnp.concatenate([(g_all * m).astype(BF16) for m in lanes], axis=0)
        logits = lax.dot_general(keys, q, NT, preferred_element_type=F32)
        power = jnp.exp(logits - jnp.max(logits, axis=0, keepdims=True))
        share = power * (1.0 / jnp.sum(power, axis=0, keepdims=True))
        share_b = share.astype(BF16)
        dshare = lax.dot_general(values, g, NT, preferred_element_type=F32)
        dot = jnp.sum(dshare * share, axis=0, keepdims=True)
        dlogits = (share * (dshare - dot)).astype(BF16)
        mixed_t = jnp.zeros((128, chunk), F32)
        dq_t = jnp.zeros((128, chunk), F32)
        for head in range(2):
            part = slice(head * chunk, (head + 1) * chunk)
            mixed_t += jnp.dot(values_t[head], share_b[:, part], preferred_element_type=F32)
            dq_t += jnp.dot(keys_t[head], dlogits[:, part], preferred_element_type=F32)
        dv = jnp.dot(share_b, g, preferred_element_type=F32)
        dk = jnp.dot(dlogits, q, preferred_element_type=F32)
        if at > 0:
            dv += dv_ref[...]
            dk += dk_ref[...]
        if at < steps - 1:
            dv_ref[...] = dv
            dk_ref[...] = dk
        else:
            d_ref[1] = dk.astype(BF16)
            d_ref[2] = dv.astype(BF16)
        mixed_ref[window, :] = mixed_t.T.astype(BF16)
        d_ref[0, window, :] = (dq_t * HEAD_DIM ** (-0.5)).T.astype(BF16)


def attend(qkv, grads, chunk=512):
    rows, width = grads.shape
    pairs = width // 128
    return pl.pallas_call(
        functools.partial(attend_kernel, chunk=chunk),
        grid=(pairs,),
        in_specs=[
            pl.BlockSpec((rows, 128), lambda j: (0, j)),
            pl.BlockSpec((rows, 128), lambda j: (0, pairs + j)),
            pl.BlockSpec((rows, 128), lambda j: (0, 2 * pairs + j)),
            pl.BlockSpec((rows, 128), lambda j: (0, j)),
        ],
        out_specs=[
            pl.BlockSpec((rows, 128), lambda j: (0, j)),
            pl.BlockSpec((3, rows, 128), lambda j: (0, 0, j)),
        ],
        out_shape=[
            jax.ShapeDtypeStruct((rows, width), BF16),
            jax.ShapeDtypeStruct((3, rows, width), BF16),
        ],
        scratch_shapes=[pltpu.VMEM((rows, 128), F32), pltpu.VMEM((rows, 128), F32)],
        compiler_params=params(),
        name="attend",
    )(qkv, qkv, qkv, grads)


def input_grad_kernel(d_ref, weight_ref, win_ref, cot_ref, gain_ref, out_ref, scale_ref):
    width = win_ref.shape[1]
    grad = jnp.zeros(win_ref.shape, F32)
    for part in range(3):
        grad += lax.dot_general(
            d_ref[part],
            weight_ref[:, part * width : (part + 1) * width],
            NT,
            preferred_element_type=F32,
        )
    unit, inverse = unit_of(win_ref[...].astype(F32))
    product = grad * unit

    @pl.when(pl.program_id(0) == 0)
    def _():
        scale_ref[...] = jnp.zeros_like(scale_ref)

    scale_ref[...] += jnp.sum(product, axis=0, keepdims=True)
    weighted = grad * gain_ref[...]
    branch = inverse * (
        weighted
        - jnp.mean(weighted, axis=-1, keepdims=True)
        - unit * jnp.mean(product * gain_ref[...], axis=-1, keepdims=True)
    )
    out_ref[...] = (cot_ref[...].astype(F32) + branch).astype(BF16)


def input_grad(d, weight, win, cot, gain, block=512):
    rows, width = win.shape
    tile = pl.BlockSpec((block, width), lambda i: (i, 0))
    return pl.pallas_call(
        input_grad_kernel,
        grid=(rows // block,),
        in_specs=[
            pl.BlockSpec((3, block, width), lambda i: (0, i, 0)),
            pl.BlockSpec(weight.shape, lambda i: (0, 0)),
            tile,
            tile,
            pl.BlockSpec((1, width), lambda i: (0, 0)),
        ],
        out_specs=[tile, pl.BlockSpec((1, width), lambda i: (0, 0))],
        out_shape=[
            jax.ShapeDtypeStruct((rows, width), BF16),
            jax.ShapeDtypeStruct((1, width), F32),
        ],
        compiler_params=params(),
        name="input_grad",
    )(d, weight, win, cot, gain.reshape(1, width))


def weight_grad_kernel(half_ref, normed_ref, d_ref, mixed_ref, cot_ref, out_ref):
    part = half_ref[0] * 2 + pl.program_id(0)
    middle = out_ref.shape[2]

    def emit(left, right):
        grad = lax.dot_general(left, right, TN, preferred_element_type=F32).astype(BF16)
        out_ref[0] = grad[:, :middle]
        out_ref[1] = grad[:, middle:]

    @pl.when(part < 3)
    def _():
        emit(normed_ref[...], d_ref[0])

    @pl.when(part == 3)
    def _():
        emit(mixed_ref[...], cot_ref[...])


def weight_grad(half, normed, d, mixed, cot):
    rows, width = normed.shape
    whole = pl.BlockSpec((rows, width), lambda j, half: (0, 0))
    return pl.pallas_call(
        weight_grad_kernel,
        grid_spec=pltpu.PrefetchScalarGridSpec(
            num_scalar_prefetch=1,
            grid=(2,),
            in_specs=[
                whole,
                pl.BlockSpec(
                    (1, rows, width), lambda j, half: (jnp.minimum(half[0] * 2 + j, 2), 0, 0)
                ),
                whole,
                whole,
            ],
            out_specs=pl.BlockSpec((2, width, width // 2), lambda j, half: (j, 0, 0)),
        ),
        out_shape=jax.ShapeDtypeStruct((4, width, width // 2), BF16),
        compiler_params=params(),
        name="weight_grad",
    )(half.reshape(1), normed, d, mixed, cot)


def return_kernel(
    sizes, count, q_ref, s_ref, back_ref, out_ref, t_ref, arrived_ref,
    band, in_x, in_z, small, small_core, small_y, small_z, small_x,
    send_sem, recv_sem, small_send, small_recv, slot_sems, own_sem,
):
    nx, ny, nz = sizes
    rows, part_w = q_ref.shape
    half_w = part_w * ny
    band_h, piece_h = rows // nx, rows // nx // nz
    me = lax.axis_index("pts")
    y = lax.axis_index("rep")
    core = lax.rem(me, 2)
    z = lax.rem(me // 2, nz)
    x = me // (2 * nz)

    def at(x_, y_, z_, core_):
        return {"pts": (x_ * nz + z_) * 2 + core_, "rep": y_}

    by_core = [(at(x, y, z, 1 - core), 1 - core)]
    by_y = [(at(x, lax.rem(y + k, ny), z, core), lax.rem(y + k, ny)) for k in range(1, ny)]
    by_z = [(at(x, y, lax.rem(z + k, nz), core), lax.rem(z + k, nz)) for k in range(1, nz)]
    by_x = [(at(lax.rem(x + k, nx), y, z, core), lax.rem(x + k, nx)) for k in range(1, nx)]
    barrier = pltpu.get_barrier_semaphore()

    def greet(k, carry):
        pl.semaphore_signal(
            barrier, inc=1, device_id={"pts": lax.rem(me + k, count)}, device_id_type=MESH
        )
        return carry

    lax.fori_loop(1, count, greet, 0)
    for device, _ in by_y:
        pl.semaphore_signal(barrier, inc=1, device_id=device, device_id_type=MESH)
    pl.semaphore_wait(barrier, count - 1 + len(by_y))

    def slot_copy(j):
        near = j // 2 + 1
        k = near + lax.rem(j, 2) * (count - 2 * near)
        peer = lax.rem(me + k, count)
        return pltpu.make_async_remote_copy(
            src_ref=back_ref.at[peer], dst_ref=arrived_ref.at[me],
            send_sem=slot_sems.at[0, k], recv_sem=slot_sems.at[1, k],
            device_id={"pts": peer}, device_id_type=MESH,
        )

    batches, lead = BATCHES, LEAD
    edges = [(count - 1) * b // batches for b in range(batches + 1)]

    def start_slot(j, carry):
        slot_copy(j).start()
        return carry

    def sent_slot(j, carry):
        slot_copy(j).wait_send()
        return carry

    def came_slot(j, carry):
        slot_copy(j).wait_recv()
        return carry

    def issue(b):
        lax.fori_loop(edges[b], edges[b + 1], start_slot, 0)

    def drain(b):
        lax.fori_loop(edges[b], edges[b + 1], sent_slot, 0)

    done = [0]

    def advance():
        if done[0] + lead < batches:
            drain(done[0])
            issue(done[0] + lead)
            done[0] += 1

    used = [0]
    small_used = [0]

    def send(src, dst, device):
        slot = used[0]
        used[0] += 1
        copy = pltpu.make_async_remote_copy(
            src_ref=src, dst_ref=dst, send_sem=send_sem.at[slot], recv_sem=recv_sem.at[slot],
            device_id=device, device_id_type=MESH,
        )
        copy.start()
        return copy

    def send_small(peers, slots, mine):
        slots[mine] = small[...]
        copies = []
        for device, _ in peers:
            slot = small_used[0]
            small_used[0] += 1
            copy = pltpu.make_async_remote_copy(
                src_ref=small, dst_ref=slots.at[mine],
                send_sem=small_send.at[slot], recv_sem=small_recv.at[slot],
                device_id=device, device_id_type=MESH,
            )
            copy.start()
            copies.append(copy)
        return copies

    def add_small(copies, slots):
        for copy in copies:
            copy.wait()
        total = slots[0]
        for k in range(1, slots.shape[0]):
            total += slots[k]
        small[...] = total

    def columns(index, width):
        return pl.ds(pl.multiple_of(index * width, width), width)

    def lines(index, height):
        return pl.ds(pl.multiple_of(index * height, height), height)

    small[...] = s_ref[...]
    copies = [
        send(q_ref.at[lines(i, band_h), :], in_x.at[k], device) for k, (device, i) in enumerate(by_x)
    ]
    small_copies = send_small(by_x, small_x, x)
    own_slot = pltpu.make_async_copy(back_ref.at[me], arrived_ref.at[me], own_sem)
    own_slot.start()
    for b in range(lead):
        issue(b)
    for copy in copies:
        copy.wait()
    total = q_ref[lines(x, band_h), :].astype(F32)
    for k in range(nx - 1):
        total += in_x[k].astype(F32)
    band[...] = total.astype(BF16)
    copies = [
        send(band.at[lines(i, piece_h), :], in_z.at[k], device) for k, (device, i) in enumerate(by_z)
    ]
    add_small(small_copies, small_x)
    small_copies = send_small(by_z, small_z, z)
    advance()
    for copy in copies:
        copy.wait()
    total = band[lines(z, piece_h), :].astype(F32)
    for k in range(nz - 1):
        total += in_z[k].astype(F32)

    column = columns(core * ny + y, part_w)
    first = pl.multiple_of(x * band_h + z * piece_h, piece_h)
    out_ref[pl.ds(first, piece_h), column] = total.astype(BF16)

    def spread(peers, view):
        return [send(view, view, device) for device, _ in peers]

    copies = spread(by_z, out_ref.at[pl.ds(first, piece_h), column])
    add_small(small_copies, small_z)
    small_copies = send_small(by_y, small_y, y)
    advance()
    for copy in copies:
        copy.wait()
    copies = spread(by_x, out_ref.at[lines(x, band_h), column])
    add_small(small_copies, small_y)
    small_copies = send_small(by_core, small_core, core)
    advance()
    for copy in copies:
        copy.wait()
    own = out_ref.at[:, column]
    if ny == 4:
        turn = 1 - 2 * core
        ahead = at(x, lax.rem(y + turn + ny, ny), z, core)
        behind = at(x, lax.rem(y - turn + ny, ny), z, core)

        def block(step):
            return out_ref.at[:, columns(core * ny + lax.rem(y + step * turn + ny, ny), part_w)]

        forth, back = send(own, own, ahead), send(own, own, behind)
        last = spread(by_core, own)
        advance()
        forth.wait()
        passed = send(block(-1), block(-1), ahead)
        last += spread(by_core, block(-1))
        add_small(small_copies, small_core)
        t_ref[...] = small[...]
        advance()
        back.wait()
        last += spread(by_core, block(1))
        passed.wait()
        last += spread(by_core, block(2))
    else:
        copies = spread(by_y, own)
        add_small(small_copies, small_core)
        t_ref[...] = small[...]
        advance()
        advance()
        for copy in copies:
            copy.wait()
        last = spread(by_core, out_ref.at[:, columns(core, half_w)])
    advance()
    advance()
    for copy in last:
        copy.wait()
    own_slot.wait()
    for b in range(done[0], batches):
        drain(b)
    lax.fori_loop(0, count - 1, came_slot, 0)


def give_back(quarter, small, back, sizes):
    nx, ny, nz = sizes
    rows, part = quarter.shape
    count = back.shape[0]
    peers = 1 + (ny - 1) + (nz - 1) + (nx - 1)
    vmem = pl.BlockSpec(memory_space=pltpu.VMEM)
    anywhere = pl.BlockSpec(memory_space=pl.ANY)
    buffers = [
        (rows // nx, part), (max(nx - 1, 1), rows // nx, part), (nz - 1, rows // nx // nz, part),
    ]
    return pl.pallas_call(
        functools.partial(return_kernel, sizes, count),
        in_specs=[vmem, vmem, anywhere],
        out_specs=[vmem, vmem, anywhere],
        out_shape=[
            jax.ShapeDtypeStruct((rows, part * ny * 2), BF16),
            jax.ShapeDtypeStruct(small.shape, F32),
            jax.ShapeDtypeStruct(back.shape, BF16),
        ],
        scratch_shapes=[pltpu.VMEM(shape, BF16) for shape in buffers]
        + [pltpu.VMEM(small.shape, F32)]
        + [pltpu.VMEM((n,) + small.shape, F32) for n in (2, ny, nz, nx)]
        + [
            pltpu.SemaphoreType.DMA((2 * peers + ny,)),
            pltpu.SemaphoreType.DMA((2 * peers + ny,)),
            pltpu.SemaphoreType.DMA((peers,)),
            pltpu.SemaphoreType.DMA((peers,)),
            pltpu.SemaphoreType.DMA((2, count)),
            pltpu.SemaphoreType.DMA,
        ],
        compiler_params=params(collective_id=0, has_side_effects=True),
        name="give_back",
    )(quarter, small, back)


def scatter_core(normed, d, mixed, cot):
    pts = lax.axis_size("pts")
    core = lax.rem(lax.axis_index("pts"), 2)
    swap = [(source, source ^ 1) for source in range(pts)]
    sent = weight_grad(1 - core, normed, d, mixed, cot)
    theirs = lax.ppermute(sent, "pts", swap)
    return (
        weight_grad(core, normed, d, mixed, cot).astype(F32) + theirs.astype(F32)
    ).astype(BF16)


def scatter_rep(half):
    reps = lax.axis_size("rep")
    y = lax.axis_index("rep")

    def piece(step):
        return lax.dynamic_index_in_dim(half, lax.rem(y + step, reps), 0, keepdims=False)

    total = piece(0).astype(F32)
    for step in range(1, reps):
        total += shifted(piece(step), "rep", step).astype(F32)
    return total.astype(BF16)


def route_slots(rank_row, point_count, total, row_count, shard_count, send_size, offset):
    slot_total = rank_row.shape[0]
    index = jnp.arange(slot_total, dtype=jnp.int32)
    live_slot = index < point_count
    moved = rank_row % total
    target_shard = jnp.where(live_slot, moved // row_count, shard_count)
    matches = target_shard[:, None] == jnp.arange(shard_count, dtype=jnp.int32)[None, :]
    earlier = (index[:, None] > index[None, :]).astype(BF16)
    before = jnp.dot(earlier, matches.astype(BF16), preferred_element_type=F32)
    ordinal = jnp.sum(jnp.where(matches, before, 0.0), axis=1).astype(jnp.int32)
    target = jnp.where(live_slot, target_shard * send_size + ordinal, shard_count * send_size)
    position = (moved % row_count - offset) % row_count
    here = (ordinal[:, None] == jnp.arange(send_size, dtype=jnp.int32)[None, :]) & live_slot[:, None]
    digits = jnp.concatenate(
        [
            jnp.where(here, digit[:, None], 0).astype(BF16)
            for digit in (position // 32, position % 32, jnp.ones_like(position))
        ],
        axis=1,
    )
    found = lax.dot_general(matches.astype(BF16), digits, TN, preferred_element_type=F32)
    high, low, live = jnp.split(found, 3, axis=1)
    return target, jnp.where(live > 0.5, high * 32 + low, -1.0).astype(jnp.int32)


def on_device(
    sizes, points, counts, hilbert_rank, patch_shift, norm_gain, project_in, project_out, cotangent
):
    shard_count = lax.axis_size("pts")
    row_count = cotangent.shape[1]
    width = points.shape[2]
    slot_total = points.shape[1]
    slot_size = slot_total // shard_count
    total = row_count * shard_count
    offset = patch_shift[0]
    limit = row_count - offset
    own_row = jnp.arange(row_count, dtype=jnp.int32)[:, None] < limit

    cot_rows = cotangent[0]
    cot_next = shifted(cot_rows, "pts", -1)

    target, out_position = route_slots(
        hilbert_rank[0], counts[0, 0], total, row_count, shard_count, slot_size, offset
    )
    outgoing = place(target, points[0], slot_total)
    outgoing, cot_next = lax.optimization_barrier((outgoing, cot_next))
    lanes = -(-slot_size // 128) * 128
    sent_position = jnp.pad(
        out_position.reshape(shard_count, 1, slot_size),
        ((0, 0), (0, 0), (0, lanes - slot_size)),
        constant_values=-1,
    )
    incoming, in_position = deliver(
        outgoing.reshape(shard_count, slot_size, width), sent_position
    )
    incoming = incoming.reshape(slot_total, width)
    in_position = in_position[:, 0, :slot_size].reshape(slot_total)

    cot_window = lax.dynamic_slice_in_dim(
        jnp.concatenate([cot_rows, cot_next], axis=0), offset, row_count, 0
    )
    grad_mixed = jnp.dot(cot_window, project_out.T, preferred_element_type=F32).astype(BF16)

    rolled = place(in_position, incoming, row_count)
    rolled_next = shifted(rolled, "pts", -1)
    target_column = target.reshape(slot_total, 1)
    position_column = jnp.maximum(in_position, -1).reshape(slot_total, 1)
    rolled_next, target_column, position_column, grad_mixed = lax.optimization_barrier(
        (rolled_next, target_column, position_column, grad_mixed)
    )
    window, normed, qkv = project(limit.reshape(1), rolled, rolled_next, norm_gain, project_in)
    mixed, d_qkv = attend(qkv, grad_mixed)
    grad_window, scale = input_grad(d_qkv, project_in, window, cot_window, norm_gain)
    grad_back = shifted(grad_window, "pts", 1)

    half = scatter_core(normed, d_qkv, mixed, cot_window)
    block_window = (
        window.astype(F32) + jnp.dot(mixed, project_out, preferred_element_type=F32)
    ).astype(BF16)
    small = jnp.pad(scale.reshape(width // 128, 128), ((0, 8 - width // 128), (0, 0)))
    grad_back, half, block_window, position_column, small = lax.optimization_barrier(
        (grad_back, half, block_window, position_column, small)
    )
    quarter = scatter_rep(half)
    block_back = shifted(block_window, "pts", 1)

    grad_rolled = jnp.where(own_row, grad_window, grad_back)
    returning = fetch(position_column, grad_rolled)
    summed, small, arrived = give_back(
        quarter, small, returning.reshape(shard_count, slot_size, width), sizes
    )
    arrived = arrived.reshape(slot_total, width)

    factor = 1.0 / math.sqrt(total * lax.axis_size("rep"))
    grad_points, grad_in, grad_out, block_rows = finish(
        offset.reshape(1), target_column, arrived, summed, block_window, block_back, factor
    )
    return (
        block_rows[None],
        grad_points[None],
        grad_in,
        grad_out,
        small[: width // 128].reshape(width) * factor,
    )


def solution(mesh):
    spread = mesh.shape["pts"]
    sizes = {64: (4, 4, 8), 8: (2, 2, 2), 4: (1, 4, 2)}[spread]
    return jax.shard_map(
        functools.partial(on_device, sizes),
        mesh=mesh,
        in_specs=(
            P("rep", "pts", None),
            P("rep", "pts"),
            P("rep", "pts"),
            P("rep"),
            P(),
            P(),
            P(),
            P("rep", "pts", None),
        ),
        out_specs=(P("rep", "pts", None), P("rep", "pts", None), P(), P(), P()),
        check_vma=False,
    )
```

```python
import functools
import math

import jax
import jax.numpy as jnp
from jax import lax
from jax.experimental import pallas as pl
from jax.experimental.pallas import tpu as pltpu
from jax.sharding import PartitionSpec as P


HEAD_DIM = 64
EPSILON = 1e-05
MESH = pl.DeviceIdType.MESH
BATCHES = 9
LEAD = 4
BF16 = jnp.bfloat16
F32 = jnp.float32
NT = (((1,), (1,)), ((), ()))
TN = (((0,), (0,)), ((), ()))


def params(**kw):
    return pltpu.CompilerParams(vmem_limit_bytes=56 << 20, **kw)


def shifted(value, axis, steps):
    count = lax.axis_size(axis)
    pairs = [(source, (source + steps) % count) for source in range(count)]
    return lax.ppermute(value, axis, pairs)


def place_kernel(dest_ref, src_ref, out_ref):
    block, depth = out_ref.shape[0], src_ref.shape[0]
    row = lax.broadcasted_iota(jnp.int32, (block, depth), 0) + pl.program_id(0) * block
    hot = jnp.where(row == dest_ref[...], 1.0, 0.0).astype(BF16)
    out_ref[...] = jnp.dot(hot, src_ref[...], preferred_element_type=F32).astype(BF16)


def place(dest, src, rows, block=512):
    depth, width = src.shape
    return pl.pallas_call(
        place_kernel,
        grid=(rows // block,),
        in_specs=[
            pl.BlockSpec((1, depth), lambda i: (0, 0)),
            pl.BlockSpec((depth, width), lambda i: (0, 0)),
        ],
        out_specs=pl.BlockSpec((block, width), lambda i: (i, 0)),
        out_shape=jax.ShapeDtypeStruct((rows, width), BF16),
        compiler_params=params(),
        name="place",
    )(dest.reshape(1, depth), src)


def take(index_ref, src_ref, out_ref):
    block, depth = out_ref.shape[0], src_ref.shape[0]
    index = jnp.broadcast_to(index_ref[...].astype(F32), (128, block)).T[:, :1].astype(jnp.int32)
    column = lax.broadcasted_iota(jnp.int32, (block, depth), 1)
    hot = jnp.where(column == index, 1.0, 0.0).astype(BF16)
    out_ref[...] = jnp.dot(hot, src_ref[...], preferred_element_type=F32).astype(BF16)


def fetch_kernel(limit_ref, index_ref, own_ref, back_ref, out_ref, src_ref):
    @pl.when(pl.program_id(0) == 0)
    def _():
        row = lax.broadcasted_iota(jnp.int32, own_ref.shape, 0)
        src_ref[...] = jnp.where(
            row < limit_ref[0], own_ref[...].astype(F32), back_ref[...].astype(F32)
        ).astype(BF16)

    take(index_ref, src_ref, out_ref)


def fetch(limit, index, own, back, block=512):
    rows = index.shape[1]
    whole = pl.BlockSpec(own.shape, lambda i: (0, 0))
    return pl.pallas_call(
        fetch_kernel,
        grid=(rows // block,),
        in_specs=[
            pl.BlockSpec(memory_space=pltpu.SMEM),
            pl.BlockSpec((1, block), lambda i: (0, i)),
            whole,
            whole,
        ],
        out_specs=pl.BlockSpec((block, own.shape[1]), lambda i: (i, 0)),
        out_shape=jax.ShapeDtypeStruct((rows, own.shape[1]), BF16),
        scratch_shapes=[pltpu.VMEM(own.shape, BF16)],
        compiler_params=params(),
        name="fetch",
    )(limit, index, own, back)


def deliver_kernel(count, out_ref, pos_ref, in_ref, in_pos_ref, sems, own_sems):
    me = lax.axis_index("pts")
    barrier = pltpu.get_barrier_semaphore()

    def greet(k, carry):
        pl.semaphore_signal(
            barrier, inc=1, device_id={"pts": lax.rem(me + k, count)}, device_id_type=MESH
        )
        return carry

    lax.fori_loop(1, count, greet, 0)
    pl.semaphore_wait(barrier, count - 1)
    own = [
        pltpu.make_async_copy(pos_ref.at[me], in_pos_ref.at[me], own_sems.at[0]),
        pltpu.make_async_copy(out_ref.at[me], in_ref.at[me], own_sems.at[1]),
    ]
    for copy in own:
        copy.start()

    def copies(j):
        near = j // 2 + 1
        k = near + lax.rem(j, 2) * (count - 2 * near)
        peer = lax.rem(me + k, count)
        return [
            pltpu.make_async_remote_copy(
                src_ref=src.at[peer], dst_ref=dst.at[me],
                send_sem=sems.at[2 * row, k], recv_sem=sems.at[2 * row + 1, k],
                device_id={"pts": peer}, device_id_type=MESH,
            )
            for row, (src, dst) in enumerate(((pos_ref, in_pos_ref), (out_ref, in_ref)))
        ]

    def start(j, carry):
        for copy in copies(j):
            copy.start()
        return carry

    def finish(j, carry):
        for copy in copies(j):
            copy.wait()
        return carry

    lax.fori_loop(0, count - 1, start, 0)
    lax.fori_loop(0, count - 1, finish, 0)
    for copy in own:
        copy.wait()


def deliver(outgoing, position):
    count = outgoing.shape[0]
    anywhere = pl.BlockSpec(memory_space=pl.ANY)
    return pl.pallas_call(
        functools.partial(deliver_kernel, count),
        in_specs=[anywhere, anywhere],
        out_specs=[anywhere, anywhere],
        out_shape=[
            jax.ShapeDtypeStruct(outgoing.shape, outgoing.dtype),
            jax.ShapeDtypeStruct(position.shape, position.dtype),
        ],
        scratch_shapes=[pltpu.SemaphoreType.DMA((4, count)), pltpu.SemaphoreType.DMA((2,))],
        compiler_params=params(collective_id=1, has_side_effects=True),
        name="deliver",
    )(outgoing, position)


def finish_kernel(
    offset_ref, index_ref, src_ref, grad_ref, window_ref, back_ref, small_ref,
    out_ref, in_ref, outer_ref, block_ref, gain_ref, *, factor,
):
    take(index_ref, src_ref, out_ref)
    for line in range(gain_ref.shape[1] // 128):
        gain_ref[:, line * 128 : (line + 1) * 128] = small_ref[line : line + 1, :] * factor
    rows = window_ref.shape[0]
    row = lax.broadcasted_iota(jnp.int32, window_ref.shape, 0)
    rolled = jnp.where(
        row < rows - offset_ref[0], window_ref[...].astype(F32), back_ref[...].astype(F32)
    )
    block_ref[...] = pltpu.roll(rolled, offset_ref[0], 0).astype(BF16)
    inner = in_ref.shape[1]
    in_ref[...] = grad_ref[:, :inner].astype(F32) * factor
    outer_ref[...] = grad_ref[:, inner:].astype(F32) * factor


def finish(offset, index, src, grads, window, back, small, factor, steps=4):
    depth, width = src.shape
    rows, tall = index.shape[1], grads.shape[0]
    block, part, lanes = rows // steps, tall // steps, width // steps
    inner = grads.shape[1] - width
    strip = pl.BlockSpec((window.shape[0], lanes), lambda i: (0, i))
    return pl.pallas_call(
        functools.partial(finish_kernel, factor=factor),
        grid=(steps,),
        in_specs=[
            pl.BlockSpec(memory_space=pltpu.SMEM),
            pl.BlockSpec((1, block), lambda i: (0, i)),
            pl.BlockSpec((depth, width), lambda i: (0, 0)),
            pl.BlockSpec((part, inner + width), lambda i: (i, 0)),
            strip,
            strip,
            pl.BlockSpec(small.shape, lambda i: (0, 0)),
        ],
        out_specs=[
            pl.BlockSpec((block, width), lambda i: (i, 0)),
            pl.BlockSpec((part, inner), lambda i: (i, 0)),
            pl.BlockSpec((part, width), lambda i: (i, 0)),
            strip,
            pl.BlockSpec((1, width), lambda i: (0, 0)),
        ],
        out_shape=[
            jax.ShapeDtypeStruct((rows, width), BF16),
            jax.ShapeDtypeStruct((tall, inner), F32),
            jax.ShapeDtypeStruct((tall, width), F32),
            jax.ShapeDtypeStruct(window.shape, BF16),
            jax.ShapeDtypeStruct((1, width), F32),
        ],
        compiler_params=params(),
        name="finish",
    )(offset, index, src, grads, window, back, small)


def unit_of(values):
    centre = jnp.mean(values, axis=-1, keepdims=True)
    deviation = values - centre
    inverse = lax.rsqrt(jnp.mean(deviation * deviation, axis=-1, keepdims=True) + EPSILON)
    return deviation * inverse, inverse


def project_kernel(limit_ref, own_ref, next_ref, gain_ref, weight_ref, win_ref, normed_ref, qkv_ref):
    block = own_ref.shape[0]
    row = lax.broadcasted_iota(jnp.int32, own_ref.shape, 0) + pl.program_id(0) * block
    values = jnp.where(
        row < limit_ref[0], own_ref[...].astype(F32), next_ref[...].astype(F32)
    )
    unit, _ = unit_of(values)
    normed = (unit * gain_ref[...]).astype(BF16)
    win_ref[...] = values.astype(BF16)
    normed_ref[...] = normed
    qkv_ref[...] = jnp.dot(normed, weight_ref[...], preferred_element_type=F32).astype(BF16)


def project(limit, own, following, gain, weight, block=512):
    rows, width = own.shape
    wide = weight.shape[1]
    tile = pl.BlockSpec((block, width), lambda i: (i, 0))
    return pl.pallas_call(
        project_kernel,
        grid=(rows // block,),
        in_specs=[
            pl.BlockSpec(memory_space=pltpu.SMEM),
            tile,
            tile,
            pl.BlockSpec((1, width), lambda i: (0, 0)),
            pl.BlockSpec((width, wide), lambda i: (0, 0)),
        ],
        out_specs=[tile, tile, pl.BlockSpec((block, wide), lambda i: (i, 0))],
        out_shape=[
            jax.ShapeDtypeStruct((rows, width), BF16),
            jax.ShapeDtypeStruct((rows, width), BF16),
            jax.ShapeDtypeStruct((rows, wide), BF16),
        ],
        compiler_params=params(),
        name="project",
    )(limit, own, following, gain.reshape(1, width), weight)


def attend_kernel(q_ref, k_ref, v_ref, g_ref, mixed_ref, d_ref, dk_ref, dv_ref, *, chunk):
    rows = q_ref.shape[0]
    keys, values = k_ref[...], v_ref[...]
    lane = lax.broadcasted_iota(jnp.int32, (1, 128), 1)
    line = lax.broadcasted_iota(jnp.int32, (128, 1), 0)
    lanes = [jnp.where(lane < HEAD_DIM, 1.0, 0.0), jnp.where(lane < HEAD_DIM, 0.0, 1.0)]
    lines = [jnp.where(line < HEAD_DIM, 1.0, 0.0), jnp.where(line < HEAD_DIM, 0.0, 1.0)]
    keys_t = keys.astype(F32).T
    values_t = values.astype(F32).T
    keys_t = [(keys_t * m).astype(BF16) for m in lines]
    values_t = [(values_t * m).astype(BF16) for m in lines]
    steps = rows // chunk
    for at in range(steps):
        window = slice(at * chunk, (at + 1) * chunk)
        q_all = q_ref[window, :].astype(F32) * HEAD_DIM ** (-0.5)
        g_all = g_ref[window, :].astype(F32)
        q = jnp.concatenate([(q_all * m).astype(BF16) for m in lanes], axis=0)
        g = jnp.concatenate([(g_all * m).astype(BF16) for m in lanes], axis=0)
        logits = lax.dot_general(keys, q, NT, preferred_element_type=F32)
        power = jnp.exp(logits - jnp.max(logits, axis=0, keepdims=True))
        share = power * (1.0 / jnp.sum(power, axis=0, keepdims=True))
        share_b = share.astype(BF16)
        dshare = lax.dot_general(values, g, NT, preferred_element_type=F32)
        dot = jnp.sum(dshare * share, axis=0, keepdims=True)
        dlogits = (share * (dshare - dot)).astype(BF16)
        mixed_t = jnp.zeros((128, chunk), F32)
        dq_t = jnp.zeros((128, chunk), F32)
        for head in range(2):
            part = slice(head * chunk, (head + 1) * chunk)
            mixed_t += jnp.dot(values_t[head], share_b[:, part], preferred_element_type=F32)
            dq_t += jnp.dot(keys_t[head], dlogits[:, part], preferred_element_type=F32)
        dv = jnp.dot(share_b, g, preferred_element_type=F32)
        dk = jnp.dot(dlogits, q, preferred_element_type=F32)
        if at > 0:
            dv += dv_ref[...]
            dk += dk_ref[...]
        if at < steps - 1:
            dv_ref[...] = dv
            dk_ref[...] = dk
        else:
            d_ref[1] = dk.astype(BF16)
            d_ref[2] = dv.astype(BF16)
        mixed_ref[window, :] = mixed_t.T.astype(BF16)
        d_ref[0, window, :] = (dq_t * HEAD_DIM ** (-0.5)).T.astype(BF16)


def attend(qkv, grads, chunk=512):
    rows, width = grads.shape
    pairs = width // 128
    return pl.pallas_call(
        functools.partial(attend_kernel, chunk=chunk),
        grid=(pairs,),
        in_specs=[
            pl.BlockSpec((rows, 128), lambda j: (0, j)),
            pl.BlockSpec((rows, 128), lambda j: (0, pairs + j)),
            pl.BlockSpec((rows, 128), lambda j: (0, 2 * pairs + j)),
            pl.BlockSpec((rows, 128), lambda j: (0, j)),
        ],
        out_specs=[
            pl.BlockSpec((rows, 128), lambda j: (0, j)),
            pl.BlockSpec((3, rows, 128), lambda j: (0, 0, j)),
        ],
        out_shape=[
            jax.ShapeDtypeStruct((rows, width), BF16),
            jax.ShapeDtypeStruct((3, rows, width), BF16),
        ],
        scratch_shapes=[pltpu.VMEM((rows, 128), F32), pltpu.VMEM((rows, 128), F32)],
        compiler_params=params(),
        name="attend",
    )(qkv, qkv, qkv, grads)


def input_grad_kernel(d_ref, weight_ref, win_ref, cot_ref, gain_ref, out_ref, scale_ref):
    width = win_ref.shape[1]
    grad = jnp.zeros(win_ref.shape, F32)
    for part in range(3):
        grad += lax.dot_general(
            d_ref[part],
            weight_ref[:, part * width : (part + 1) * width],
            NT,
            preferred_element_type=F32,
        )
    unit, inverse = unit_of(win_ref[...].astype(F32))
    product = grad * unit

    @pl.when(pl.program_id(0) == 0)
    def _():
        scale_ref[...] = jnp.zeros_like(scale_ref)

    scale_ref[...] += jnp.sum(product, axis=0, keepdims=True)
    weighted = grad * gain_ref[...]
    branch = inverse * (
        weighted
        - jnp.mean(weighted, axis=-1, keepdims=True)
        - unit * jnp.mean(product * gain_ref[...], axis=-1, keepdims=True)
    )
    out_ref[...] = (cot_ref[...].astype(F32) + branch).astype(BF16)


def input_grad(d, weight, win, cot, gain, block=512):
    rows, width = win.shape
    tile = pl.BlockSpec((block, width), lambda i: (i, 0))
    return pl.pallas_call(
        input_grad_kernel,
        grid=(rows // block,),
        in_specs=[
            pl.BlockSpec((3, block, width), lambda i: (0, i, 0)),
            pl.BlockSpec(weight.shape, lambda i: (0, 0)),
            tile,
            tile,
            pl.BlockSpec((1, width), lambda i: (0, 0)),
        ],
        out_specs=[tile, pl.BlockSpec((1, width), lambda i: (0, 0))],
        out_shape=[
            jax.ShapeDtypeStruct((rows, width), BF16),
            jax.ShapeDtypeStruct((1, width), F32),
        ],
        compiler_params=params(),
        name="input_grad",
    )(d, weight, win, cot, gain.reshape(1, width))


def weight_grad_kernel(half_ref, normed_ref, d_ref, mixed_ref, cot_ref, out_ref):
    part = half_ref[0] * 2 + pl.program_id(0)
    middle = out_ref.shape[2]

    def emit(left, right):
        grad = lax.dot_general(left, right, TN, preferred_element_type=F32).astype(BF16)
        out_ref[0] = grad[:, :middle]
        out_ref[1] = grad[:, middle:]

    @pl.when(part < 3)
    def _():
        emit(normed_ref[...], d_ref[0])

    @pl.when(part == 3)
    def _():
        emit(mixed_ref[...], cot_ref[...])


def weight_grad(half, normed, d, mixed, cot):
    rows, width = normed.shape
    whole = pl.BlockSpec((rows, width), lambda j, half: (0, 0))
    return pl.pallas_call(
        weight_grad_kernel,
        grid_spec=pltpu.PrefetchScalarGridSpec(
            num_scalar_prefetch=1,
            grid=(2,),
            in_specs=[
                whole,
                pl.BlockSpec(
                    (1, rows, width), lambda j, half: (jnp.minimum(half[0] * 2 + j, 2), 0, 0)
                ),
                whole,
                whole,
            ],
            out_specs=pl.BlockSpec((2, width, width // 2), lambda j, half: (j, 0, 0)),
        ),
        out_shape=jax.ShapeDtypeStruct((4, width, width // 2), BF16),
        compiler_params=params(),
        name="weight_grad",
    )(half.reshape(1), normed, d, mixed, cot)


def return_kernel(sizes, count, *refs):
    nx, ny, nz = sizes
    parts = refs[:ny]
    (
        s_ref, back_ref, out_ref, t_ref, arrived_ref,
        q_ref, band, in_x, in_z, small, small_core, small_y, small_z, small_x,
        send_sem, recv_sem, small_send, small_recv, slot_sems, own_sem,
    ) = refs[ny:]
    rows, part_w = q_ref.shape
    half_w = part_w * ny
    band_h, piece_h = rows // nx, rows // nx // nz
    me = lax.axis_index("pts")
    y = lax.axis_index("rep")
    core = lax.rem(me, 2)
    z = lax.rem(me // 2, nz)
    x = me // (2 * nz)

    def at(x_, y_, z_, core_):
        return {"pts": (x_ * nz + z_) * 2 + core_, "rep": y_}

    by_core = [(at(x, y, z, 1 - core), 1 - core)]
    by_y = [(at(x, lax.rem(y + k, ny), z, core), lax.rem(y + k, ny)) for k in range(1, ny)]
    by_z = [(at(x, y, lax.rem(z + k, nz), core), lax.rem(z + k, nz)) for k in range(1, nz)]
    by_x = [(at(lax.rem(x + k, nx), y, z, core), lax.rem(x + k, nx)) for k in range(1, nx)]
    barrier = pltpu.get_barrier_semaphore()

    def greet(k, carry):
        pl.semaphore_signal(
            barrier, inc=1, device_id={"pts": lax.rem(me + k, count)}, device_id_type=MESH
        )
        return carry

    lax.fori_loop(1, count, greet, 0)
    for device, _ in by_y:
        pl.semaphore_signal(barrier, inc=1, device_id=device, device_id_type=MESH)
    total = parts[0][...].astype(F32)
    for k in range(1, ny):
        total += parts[k][...].astype(F32)
    q_ref[...] = total.astype(BF16)
    small[...] = s_ref[...]
    pl.semaphore_wait(barrier, count - 1 + len(by_y))

    def slot_copy(j):
        near = j // 2 + 1
        k = near + lax.rem(j, 2) * (count - 2 * near)
        peer = lax.rem(me + k, count)
        return pltpu.make_async_remote_copy(
            src_ref=back_ref.at[peer], dst_ref=arrived_ref.at[me],
            send_sem=slot_sems.at[0, k], recv_sem=slot_sems.at[1, k],
            device_id={"pts": peer}, device_id_type=MESH,
        )

    batches, lead = BATCHES, LEAD
    edges = [(count - 1) * b // batches for b in range(batches + 1)]

    def start_slot(j, carry):
        slot_copy(j).start()
        return carry

    def sent_slot(j, carry):
        slot_copy(j).wait_send()
        return carry

    def came_slot(j, carry):
        slot_copy(j).wait_recv()
        return carry

    def issue(b):
        lax.fori_loop(edges[b], edges[b + 1], start_slot, 0)

    def drain(b):
        lax.fori_loop(edges[b], edges[b + 1], sent_slot, 0)

    done = [0]

    def advance():
        if done[0] + lead < batches:
            drain(done[0])
            issue(done[0] + lead)
            done[0] += 1

    used = [0]
    small_used = [0]

    def send(src, dst, device):
        slot = used[0]
        used[0] += 1
        copy = pltpu.make_async_remote_copy(
            src_ref=src, dst_ref=dst, send_sem=send_sem.at[slot], recv_sem=recv_sem.at[slot],
            device_id=device, device_id_type=MESH,
        )
        copy.start()
        return copy

    def send_small(peers, slots, mine):
        slots[mine] = small[...]
        copies = []
        for device, _ in peers:
            slot = small_used[0]
            small_used[0] += 1
            copy = pltpu.make_async_remote_copy(
                src_ref=small, dst_ref=slots.at[mine],
                send_sem=small_send.at[slot], recv_sem=small_recv.at[slot],
                device_id=device, device_id_type=MESH,
            )
            copy.start()
            copies.append(copy)
        return copies

    def add_small(copies, slots):
        for copy in copies:
            copy.wait()
        total = slots[0]
        for k in range(1, slots.shape[0]):
            total += slots[k]
        small[...] = total

    def columns(index, width):
        return pl.ds(pl.multiple_of(index * width, width), width)

    def lines(index, height):
        return pl.ds(pl.multiple_of(index * height, height), height)

    copies = [
        send(q_ref.at[lines(i, band_h), :], in_x.at[k], device) for k, (device, i) in enumerate(by_x)
    ]
    small_copies = send_small(by_x, small_x, x)
    own_slot = pltpu.make_async_copy(back_ref.at[me], arrived_ref.at[me], own_sem)
    own_slot.start()
    for b in range(lead):
        issue(b)
    for copy in copies:
        copy.wait()
    total = q_ref[lines(x, band_h), :].astype(F32)
    for k in range(nx - 1):
        total += in_x[k].astype(F32)
    band[...] = total.astype(BF16)
    copies = [
        send(band.at[lines(i, piece_h), :], in_z.at[k], device) for k, (device, i) in enumerate(by_z)
    ]
    add_small(small_copies, small_x)
    small_copies = send_small(by_z, small_z, z)
    advance()
    for copy in copies:
        copy.wait()
    total = band[lines(z, piece_h), :].astype(F32)
    for k in range(nz - 1):
        total += in_z[k].astype(F32)

    column = columns(core * ny + y, part_w)
    first = pl.multiple_of(x * band_h + z * piece_h, piece_h)
    out_ref[pl.ds(first, piece_h), column] = total.astype(BF16)

    def spread(peers, view):
        return [send(view, view, device) for device, _ in peers]

    copies = spread(by_z, out_ref.at[pl.ds(first, piece_h), column])
    add_small(small_copies, small_z)
    small_copies = send_small(by_y, small_y, y)
    advance()
    for copy in copies:
        copy.wait()
    copies = spread(by_x, out_ref.at[lines(x, band_h), column])
    add_small(small_copies, small_y)
    small_copies = send_small(by_core, small_core, core)
    advance()
    for copy in copies:
        copy.wait()
    own = out_ref.at[:, column]
    if ny == 4:
        turn = 1 - 2 * core
        ahead = at(x, lax.rem(y + turn + ny, ny), z, core)
        behind = at(x, lax.rem(y - turn + ny, ny), z, core)

        def block(step):
            return out_ref.at[:, columns(core * ny + lax.rem(y + step * turn + ny, ny), part_w)]

        forth, back = send(own, own, ahead), send(own, own, behind)
        last = spread(by_core, own)
        advance()
        forth.wait()
        passed = send(block(-1), block(-1), ahead)
        last += spread(by_core, block(-1))
        add_small(small_copies, small_core)
        t_ref[...] = small[...]
        advance()
        back.wait()
        last += spread(by_core, block(1))
        passed.wait()
        last += spread(by_core, block(2))
    else:
        copies = spread(by_y, own)
        add_small(small_copies, small_core)
        t_ref[...] = small[...]
        advance()
        advance()
        for copy in copies:
            copy.wait()
        last = spread(by_core, out_ref.at[:, columns(core, half_w)])
    advance()
    advance()
    for copy in last:
        copy.wait()
    own_slot.wait()
    for b in range(done[0], batches):
        drain(b)
    lax.fori_loop(0, count - 1, came_slot, 0)


def give_back(parts, small, back, sizes):
    nx, ny, nz = sizes
    rows, part = parts[0].shape
    count = back.shape[0]
    peers = 1 + (ny - 1) + (nz - 1) + (nx - 1)
    vmem = pl.BlockSpec(memory_space=pltpu.VMEM)
    anywhere = pl.BlockSpec(memory_space=pl.ANY)
    buffers = [
        (rows, part),
        (rows // nx, part), (max(nx - 1, 1), rows // nx, part), (nz - 1, rows // nx // nz, part),
    ]
    return pl.pallas_call(
        functools.partial(return_kernel, sizes, count),
        in_specs=[vmem] * (ny + 1) + [anywhere],
        out_specs=[vmem, vmem, anywhere],
        out_shape=[
            jax.ShapeDtypeStruct((rows, part * ny * 2), BF16),
            jax.ShapeDtypeStruct(small.shape, F32),
            jax.ShapeDtypeStruct(back.shape, BF16),
        ],
        scratch_shapes=[pltpu.VMEM(shape, BF16) for shape in buffers]
        + [pltpu.VMEM(small.shape, F32)]
        + [pltpu.VMEM((n,) + small.shape, F32) for n in (2, ny, nz, nx)]
        + [
            pltpu.SemaphoreType.DMA((2 * peers + ny,)),
            pltpu.SemaphoreType.DMA((2 * peers + ny,)),
            pltpu.SemaphoreType.DMA((peers,)),
            pltpu.SemaphoreType.DMA((peers,)),
            pltpu.SemaphoreType.DMA((2, count)),
            pltpu.SemaphoreType.DMA,
        ],
        compiler_params=params(collective_id=0, has_side_effects=True),
        name="give_back",
    )(*parts, small, back)


def scatter_core(normed, d, mixed, cot):
    pts = lax.axis_size("pts")
    core = lax.rem(lax.axis_index("pts"), 2)
    swap = [(source, source ^ 1) for source in range(pts)]
    sent = weight_grad(1 - core, normed, d, mixed, cot)
    theirs = lax.ppermute(sent, "pts", swap)
    return (
        weight_grad(core, normed, d, mixed, cot).astype(F32) + theirs.astype(F32)
    ).astype(BF16)


def scatter_rep(half):
    reps = lax.axis_size("rep")
    y = lax.axis_index("rep")

    def piece(step):
        return lax.dynamic_index_in_dim(half, lax.rem(y + step, reps), 0, keepdims=False)

    return [piece(0)] + [shifted(piece(step), "rep", step) for step in range(1, reps)]


def route_slots(rank_row, point_count, total, row_count, shard_count, send_size, offset):
    slot_total = rank_row.shape[0]
    index = jnp.arange(slot_total, dtype=jnp.int32)
    live_slot = index < point_count
    moved = rank_row % total
    target_shard = jnp.where(live_slot, moved // row_count, shard_count)
    matches = target_shard[:, None] == jnp.arange(shard_count, dtype=jnp.int32)[None, :]
    earlier = (index[:, None] > index[None, :]).astype(BF16)
    before = jnp.dot(earlier, matches.astype(BF16), preferred_element_type=F32)
    ordinal = jnp.sum(jnp.where(matches, before, 0.0), axis=1).astype(jnp.int32)
    target = jnp.where(live_slot, target_shard * send_size + ordinal, shard_count * send_size)
    position = (moved % row_count - offset) % row_count
    here = (ordinal[:, None] == jnp.arange(send_size, dtype=jnp.int32)[None, :]) & live_slot[:, None]
    digits = jnp.concatenate(
        [
            jnp.where(here, digit[:, None], 0).astype(BF16)
            for digit in (position // 32, position % 32, jnp.ones_like(position))
        ],
        axis=1,
    )
    found = lax.dot_general(matches.astype(BF16), digits, TN, preferred_element_type=F32)
    high, low, live = jnp.split(found, 3, axis=1)
    return target, jnp.where(live > 0.5, high * 32 + low, -1.0).astype(jnp.int32)


def on_device(
    sizes, points, counts, hilbert_rank, patch_shift, norm_gain, project_in, project_out, cotangent
):
    shard_count = lax.axis_size("pts")
    row_count = cotangent.shape[1]
    width = points.shape[2]
    slot_total = points.shape[1]
    slot_size = slot_total // shard_count
    total = row_count * shard_count
    offset = patch_shift[0]
    limit = row_count - offset

    cot_rows = cotangent[0]
    cot_next = shifted(cot_rows, "pts", -1)

    target, out_position = route_slots(
        hilbert_rank[0], counts[0, 0], total, row_count, shard_count, slot_size, offset
    )
    outgoing = place(target, points[0], slot_total)
    outgoing, cot_next = lax.optimization_barrier((outgoing, cot_next))
    lanes = -(-slot_size // 128) * 128
    sent_position = jnp.pad(
        out_position.reshape(shard_count, 1, slot_size),
        ((0, 0), (0, 0), (0, lanes - slot_size)),
        constant_values=-1,
    )
    incoming, in_position = deliver(
        outgoing.reshape(shard_count, slot_size, width), sent_position
    )
    incoming = incoming.reshape(slot_total, width)
    in_position = in_position[:, 0, :slot_size].reshape(slot_total)

    cot_window = lax.dynamic_slice_in_dim(
        jnp.concatenate([cot_rows, cot_next], axis=0), offset, row_count, 0
    )
    grad_mixed = jnp.dot(cot_window, project_out.T, preferred_element_type=F32).astype(BF16)

    rolled = place(in_position, incoming, row_count)
    rolled_next = shifted(rolled, "pts", -1)
    rolled_next, grad_mixed = lax.optimization_barrier((rolled_next, grad_mixed))
    window, normed, qkv = project(limit.reshape(1), rolled, rolled_next, norm_gain, project_in)
    mixed, d_qkv = attend(qkv, grad_mixed)
    grad_window, scale = input_grad(d_qkv, project_in, window, cot_window, norm_gain)
    grad_back = shifted(grad_window, "pts", 1)

    half = scatter_core(normed, d_qkv, mixed, cot_window)
    block_window = (
        window.astype(F32) + jnp.dot(mixed, project_out, preferred_element_type=F32)
    ).astype(BF16)
    small = jnp.pad(scale.reshape(width // 128, 128), ((0, 8 - width // 128), (0, 0)))
    grad_back, half, block_window, small = lax.optimization_barrier(
        (grad_back, half, block_window, small)
    )
    parts = scatter_rep(half)
    block_back = shifted(block_window, "pts", 1)

    returning = fetch(limit.reshape(1), in_position.reshape(1, slot_total), grad_window, grad_back)
    summed, small, arrived = give_back(
        parts, small, returning.reshape(shard_count, slot_size, width), sizes
    )
    arrived = arrived.reshape(slot_total, width)

    factor = 1.0 / math.sqrt(total * lax.axis_size("rep"))
    grad_points, grad_in, grad_out, block_rows, gain = finish(
        offset.reshape(1), target.reshape(1, slot_total), arrived, summed,
        block_window, block_back, small, factor,
    )
    return (
        block_rows[None],
        grad_points[None],
        grad_in,
        grad_out,
        gain.reshape(width),
    )


def solution(mesh):
    spread = mesh.shape["pts"]
    sizes = {64: (4, 4, 8), 8: (2, 2, 2), 4: (1, 4, 2)}[spread]
    return jax.shard_map(
        functools.partial(on_device, sizes),
        mesh=mesh,
        in_specs=(
            P("rep", "pts", None),
            P("rep", "pts"),
            P("rep", "pts"),
            P("rep"),
            P(),
            P(),
            P(),
            P("rep", "pts", None),
        ),
        out_specs=(P("rep", "pts", None), P("rep", "pts", None), P(), P(), P()),
        check_vma=False,
    )
```
